32 devices in a mesh: dp: 1, fsdp: 32 (over z, y, x, core).
Axes of the slice: x: 2, y: 2, z: 4, core: 2. Of those that a mesh axis runs over, the one named last changes fastest.
Arguments:
- hidden_states: bfloat16 [128, 4096], P(('dp', 'fsdp')), may hold values from -400 to 400
- token_ids: int32 [128], P(('dp', 'fsdp')), may hold values from 0 to 4095
- norm_gain: float32 [4096], replicated, may hold values from 0.5 to 1.5
- ref_gate_w: bfloat16 [4096, 14784], P('dp', 'fsdp'), may hold values from -0.1875 to 0.1875
- ref_up_w: bfloat16 [4096, 14784], P('dp', 'fsdp'), may hold values from -0.1875 to 0.1875
- ref_down_w: bfloat16 [14784, 4096], P('fsdp', 'dp'), may hold values from -0.09375 to 0.09375
- pol_gate_w: bfloat16 [4096, 14784], P('dp', 'fsdp'), may hold values from -0.1875 to 0.1875
- pol_up_w: bfloat16 [4096, 14784], P('dp', 'fsdp'), may hold values from -0.1875 to 0.1875
- pol_down_w: bfloat16 [14784, 4096], P('fsdp', 'dp'), may hold values from -0.09375 to 0.09375
- sample_lengths: int32 [1, 32], P('dp'), may hold values from 1 to 24, 128 in all within a row
- prompt_index: int32 [1, 32], P('dp'), may hold values from 0 to 3, as said below
- rewards: float32 [1, 32], P('dp'), may hold values from -6 to 6
Outputs:
- grad_gate: float32 [4096, 14784], P('dp', 'fsdp')
- grad_up: float32 [4096, 14784], P('dp', 'fsdp')
- grad_down: float32 [14784, 4096], P('fsdp', 'dp')
- advantage: float32 [1, 32], P('dp')
The draws below stay inside these ranges and needn't reach their ends.
Inputs may be any that keep to these rules, and one draw needn't show every extreme that they name: `prompt_index`: in each row, every prompt from 0 to 3 is answered by exactly 8 samples. `sample_lengths`: each row sums to 128.
All inputs are finite; a program needn't handle non-finite values.
Results may differ from the reference program's by a relative error of at most 0.013.
Values may be sent and summed in bfloat16 or wider, within the bound.
No kernel may reach another device: no remote copies, remote signals or barrier semaphores. Data moves between devices by JAX's collectives and lax.ppermute only.
A program may use at most 128 MiB of HBM per device.

```python
import math
import jax
import jax.numpy as jnp
import numpy as np
from jax import lax

D = 4096
FF = 14784
K = 8
SAMPLES_G = 32
GROUP_TOK = 128
MOST_LEN = 24
TOKENS = 128
N_DP = 1


def one_order(single_key):
    return jax.random.permutation(single_key, SAMPLES_G)


def draw_prompt_index(key, part):
    row_keys = jax.random.split(jax.random.fold_in(key, 17), N_DP)
    orders = jax.vmap(one_order)(row_keys)
    return (orders // K).astype(jnp.int32)


def draw_hidden_states(key, part):
    first = jax.random.fold_in(jax.random.fold_in(key, 29), 0)
    values = 0.5 * jnp.clip(jax.random.normal(first, (TOKENS, D), jnp.float32), -5.0, 5.0)
    return values.astype(jnp.bfloat16)


def place_ends(values, rng, least, top_value):
    spot = [jax.random.randint(jax.random.fold_in(rng, axis), (), 0, length) for axis, length in enumerate(values.shape)]
    main_axis = values.shape.index(max(values.shape))
    neighbour = spot[:main_axis] + [(spot[main_axis] + 1) % values.shape[main_axis]] + spot[main_axis + 1:]
    return values.at[tuple(spot)].set(least).at[tuple(neighbour)].set(top_value)


def block_levels(rng, dims, pieces, low, high):
    def one(dim, shards_of):
        steps = jax.random.uniform(jax.random.fold_in(jax.random.fold_in(rng, 6), dim), (shards_of,), jnp.float32, low / len(pieces), high / len(pieces))
        return jnp.repeat(jnp.exp(steps), dims[dim] // shards_of).reshape((-1,) + (1,) * (len(dims) - dim - 1))

    gain = one(*pieces[0])
    for cut in pieces[1:]:
        gain = gain * one(*cut)
    return gain


def length_profile(number_of, total, limit, slope):
    loads = [(1 << 20) // math.isqrt(standing ** slope) + 1 for standing in range(2, number_of + 1)]
    rest, holding = total - limit - (number_of - 1), [1] * (number_of - 1)
    while rest > 0:
        free = [i for i in range(number_of - 1) if holding[i] < limit]
        pool, budget = sum([loads[i] for i in free]), rest
        for i in free:
            more = min(limit - holding[i], max(1, budget * loads[i] // pool), rest)
            holding[i] = holding[i] + more
            rest = rest - more
    return np.array([limit] + holding)


def ragged(own_key, number_of, total, limit, lean):
    if number_of == 2:
        one = jax.random.randint(own_key, (), max(1, total - limit), min(limit, total - 1) + 1)
        return jnp.stack([one, total - one])
    tallies = jnp.asarray(length_profile(number_of, total, limit, lean), jnp.int32)
    pairs = (number_of - 1) // 2
    source_of, receiver = tallies[1:1 + 2 * pairs:2], tallies[2:2 + 2 * pairs:2]
    slack = jnp.minimum(source_of - 1, limit - receiver)
    passed = jax.random.randint(jax.random.fold_in(own_key, 1), (pairs,), 0, 1 << 20) % (slack + 1)
    tallies = tallies.at[1:1 + 2 * pairs:2].set(source_of - passed).at[2:2 + 2 * pairs:2].set(receiver + passed)
    return tallies[jax.random.permutation(jax.random.fold_in(own_key, 2), number_of)]


def noise(own_key, shape, spread, reach, pieces=(), held_as=jnp.bfloat16):
    gain = block_levels(own_key, shape, pieces, -0.22, 0.18) if pieces else 1.0
    values = jax.random.normal(own_key, shape, jnp.float32) * spread * gain
    return jnp.minimum(jnp.maximum(values, -reach), reach).astype(held_as)


def setup_inputs(seed: int = 0) -> dict:
    key_list = jax.random.split(jax.random.key(seed), 13)
    return {
        "hidden_states": draw_hidden_states(jax.random.fold_in(key_list[12], 71), 0),
        "token_ids": place_ends(jax.random.randint(key_list[1], (TOKENS,), 0, D), jax.random.fold_in(key_list[1], 1), 0, D - 1).astype(jnp.int32),
        "norm_gain": jnp.clip(1.0 + 0.1 * jax.random.normal(key_list[2], (D,), jnp.float32), 0.5, 1.5),
        "ref_gate_w": noise(key_list[3], (D, FF), (D // 4) ** -0.5, 0.1875, ((1, 32),)),
        "ref_up_w": noise(key_list[4], (D, FF), (D // 4) ** -0.5, 0.1875, ((1, 32),)),
        "ref_down_w": noise(key_list[5], (FF, D), (FF // 4) ** -0.5, 0.09375, ((0, 32),)),
        "pol_gate_w": noise(key_list[6], (D, FF), (D // 4) ** -0.5, 0.1875, ((1, 32),)),
        "pol_up_w": noise(key_list[7], (D, FF), (D // 4) ** -0.5, 0.1875, ((1, 32),)),
        "pol_down_w": noise(key_list[8], (FF, D), (FF // 4) ** -0.5, 0.09375, ((0, 32),)),
        "sample_lengths": jax.vmap(lambda own: ragged(own, SAMPLES_G, GROUP_TOK, MOST_LEN, 1))(jax.random.split(key_list[9], N_DP)).reshape((N_DP, SAMPLES_G)).astype(jnp.int32),
        "prompt_index": draw_prompt_index(jax.random.fold_in(key_list[12], 71), 0),
        "rewards": noise(key_list[11], (N_DP, SAMPLES_G), 1.0, 6.0, (), jnp.float32),
    }


EPSILON = 1e-06
KL_WEIGHT = 0.05

def normalize(states, norm_gain):
    values = states.astype(jnp.float32)
    factor = lax.rsqrt(lax.optimization_barrier(jnp.mean(values * values, axis=-1, keepdims=True)) + EPSILON)
    return (values * factor * norm_gain).astype(jnp.bfloat16)

def block_forward(normed, gate_w, up_w, down_w):
    gate_pre = jnp.dot(normed, gate_w, preferred_element_type=jnp.float32)
    up_pre = jnp.dot(normed, up_w, preferred_element_type=jnp.float32)
    hidden = (jax.nn.silu(gate_pre) * up_pre).astype(jnp.bfloat16)
    output = jnp.dot(hidden, down_w, preferred_element_type=jnp.float32)
    return (gate_pre, up_pre, hidden, output)

def token_logprob(logits, token_ids):
    row_peak = lax.optimization_barrier(jnp.max(logits, axis=-1))
    log_total = row_peak + jnp.log(lax.optimization_barrier(jnp.sum(jnp.exp(logits - row_peak[:, None]), axis=-1)))
    columns = jnp.arange(logits.shape[1], dtype=jnp.int32)
    picked = lax.optimization_barrier(jnp.sum(jnp.where(columns[None, :] == token_ids[:, None], logits, 0.0), axis=-1))
    return (picked - log_total, log_total)

def grouped_product(left_rows, right_rows, groups):
    left_groups = left_rows.reshape(groups, -1, left_rows.shape[1])
    right_groups = right_rows.reshape(groups, -1, right_rows.shape[1])

    def accumulate(running, couple):
        product = jnp.dot(couple[0].T, couple[1], preferred_element_type=jnp.float32)
        rounded = lax.optimization_barrier(product.astype(jnp.bfloat16))
        return (running + rounded.astype(jnp.float32), None)
    start_sum = jnp.zeros((left_rows.shape[1], right_rows.shape[1]), jnp.float32)
    result, _ = lax.scan(accumulate, start_sum, (left_groups, right_groups))
    return result

def reference(hidden_states, token_ids, norm_gain, ref_gate_w, ref_up_w, ref_down_w, pol_gate_w, pol_up_w, pol_down_w, sample_lengths, prompt_index, rewards):
    normed = normalize(hidden_states, norm_gain)
    states = hidden_states.astype(jnp.float32)
    _, _, _, ref_out = block_forward(normed, ref_gate_w, ref_up_w, ref_down_w)
    ref_lp, _ = token_logprob(states + ref_out, token_ids)
    gate_pre, up_pre, hidden, pol_out = block_forward(normed, pol_gate_w, pol_up_w, pol_down_w)
    logits = states + pol_out
    pol_lp, log_total = token_logprob(logits, token_ids)
    groups = sample_lengths.shape[0]
    group_tokens = hidden_states.shape[0] // groups
    sample_ends = jnp.cumsum(sample_lengths, axis=-1)
    sample_starts = sample_ends - sample_lengths
    position = jnp.arange(group_tokens, dtype=jnp.int32)
    inside = ((position[None, :, None] >= sample_starts[:, None, :]) & (position[None, :, None] < sample_ends[:, None, :])).astype(jnp.float32)
    log_gap = (pol_lp - ref_lp).reshape(groups, group_tokens)
    divergence = jnp.einsum('gt,gts->gs', log_gap, inside)
    scores = rewards - KL_WEIGHT * divergence
    same_prompt = (prompt_index[:, :, None] == prompt_index[:, None, :]).astype(jnp.float32)
    others = jnp.einsum('gst,gt->gs', same_prompt, scores) - scores
    advantage = scores - others / (K - 1)
    weight = jnp.einsum('gts,gs->gt', inside, advantage).reshape(-1)
    columns = jnp.arange(logits.shape[1], dtype=jnp.int32)
    onehot = (columns[None, :] == token_ids[:, None]).astype(jnp.float32)
    grad_logits = (-weight[:, None] * (onehot - jnp.exp(logits - log_total[:, None]))).astype(jnp.bfloat16)
    grad_hidden = lax.dot_general(grad_logits, pol_down_w, (((1,), (1,)), ((), ())), preferred_element_type=jnp.float32)
    sigmoid_gate = jax.nn.sigmoid(gate_pre)
    grad_gate_pre = (grad_hidden * up_pre * sigmoid_gate * (1.0 + gate_pre * (1.0 - sigmoid_gate))).astype(jnp.bfloat16)
    grad_up_pre = (grad_hidden * gate_pre * sigmoid_gate).astype(jnp.bfloat16)
    grad_down = grouped_product(hidden, grad_logits, groups)
    grad_inner = grouped_product(normed, jnp.concatenate([grad_gate_pre, grad_up_pre], axis=1), groups)
    unit_count = gate_pre.shape[1]
    return (grad_inner[:, :unit_count], grad_inner[:, unit_count:], grad_down, advantage)
```

```python
import jax
import jax.numpy as jnp
import numpy as np
from jax import lax
from jax.sharding import PartitionSpec as P

K = 8


EPSILON = 1e-06
KL_WEIGHT = 0.05
PIECES = 3
LANES = 128


def exchange_levels(members):
    bits = [1 << b for b in range(members.bit_length() - 1)]
    levels, rest = [bits[:1]], bits[1:]
    while rest:
        low, rest = rest[:2], rest[2:]
        levels.append(low + [low[0] | low[1]] if len(low) == 2 else low)
    return [level for level in levels if level]


def swap(values, mask):
    members = lax.axis_size("fsdp")
    return lax.ppermute(values, "fsdp", [(i, i ^ mask) for i in range(members)])


def gather_rows(rows, levels):
    for level in reversed(levels):
        rows = jnp.concatenate([rows] + [swap(rows, mask) for mask in level], axis=0)
    return rows


def scatter_rows(sums, levels):
    for level in levels:
        count = sums.shape[0] // (len(level) + 1)
        own = sums[:count]
        for place, mask in enumerate(level):
            block = sums[(place + 1) * count : (place + 2) * count]
            own = own + swap(block.astype(jnp.bfloat16), mask).astype(jnp.float32)
        sums = own
    return sums


def row_masks(levels):
    masks = np.zeros((1,), np.int32)
    for level in reversed(levels):
        masks = np.concatenate([masks] + [masks ^ mask for mask in level])
    return masks


def split_float(value):
    pieces = []
    for _ in range(PIECES):
        piece = lax.reduce_precision(value, 8, 7)
        pieces.append(piece)
        value = value - piece
    return pieces


def local_single(
    hidden_states,
    token_ids,
    norm_gain,
    ref_gate_w,
    ref_up_w,
    ref_down_w,
    pol_gate_w,
    pol_up_w,
    pol_down_w,
    sample_lengths,
    prompt_index,
    rewards,
):
    token_count, width = hidden_states.shape
    levels = exchange_levels(lax.axis_size("fsdp"))
    masks = row_masks(levels)
    tokens = token_count * masks.size
    member = lax.axis_index("fsdp").astype(jnp.int32)

    normed = normalize(gather_rows(hidden_states, levels), norm_gain)

    def forward(gate_w, up_w, down_w):
        gate_pre = jnp.dot(normed, gate_w, preferred_element_type=jnp.float32)
        up_pre = jnp.dot(normed, up_w, preferred_element_type=jnp.float32)
        hidden = (jax.nn.silu(gate_pre) * up_pre).astype(jnp.bfloat16)
        return gate_pre, up_pre, hidden, jnp.dot(hidden, down_w, preferred_element_type=jnp.float32)

    gate_pre, up_pre, hidden, pol_part = forward(pol_gate_w, pol_up_w, pol_down_w)
    _, _, _, ref_part = forward(ref_gate_w, ref_up_w, ref_down_w)
    sums = scatter_rows(jnp.concatenate([pol_part, ref_part], axis=1), levels)

    states = hidden_states.astype(jnp.float32)
    columns = jnp.arange(width, dtype=jnp.int32)
    chosen = columns[None, :] == token_ids[:, None]

    def token_logprob(logits):
        row_peak = jnp.max(logits, axis=1)
        log_total = row_peak + jnp.log(jnp.sum(jnp.exp(logits - row_peak[:, None]), axis=1))
        return jnp.sum(jnp.where(chosen, logits, 0.0), axis=1) - log_total, log_total

    logits = states + sums[:, :width]
    pol_lp, log_total = token_logprob(logits)
    ref_lp, _ = token_logprob(states + sums[:, width:])
    slopes = jnp.exp(logits - log_total[:, None]) - chosen.astype(jnp.float32)
    extra = jnp.stack(split_float(pol_lp - ref_lp), axis=1)
    extra = jnp.pad(extra, ((0, 0), (0, LANES - PIECES)))
    sent = jnp.concatenate([slopes, extra], axis=1).astype(jnp.bfloat16)
    received = gather_rows(sent, levels)
    slopes_all = received[:, :width]
    gap = jnp.sum(received[:, width : width + PIECES].astype(jnp.float32), axis=1)

    sample_ends = jnp.cumsum(sample_lengths[0])
    sample_starts = sample_ends - sample_lengths[0]

    def inside_of(position):
        return (position[:, None] >= sample_starts[None, :]) & (
            position[:, None] < sample_ends[None, :]
        )

    row_place = (
        (member ^ jnp.asarray(np.repeat(masks, token_count))) * token_count
        + jnp.asarray(np.tile(np.arange(token_count, dtype=np.int32), masks.size))
    )
    place = jnp.arange(tokens, dtype=jnp.int32)
    ordered = jnp.sum(jnp.where(place[:, None] == row_place[None, :], gap[None, :], 0.0), axis=1)
    divergence = jnp.sum(jnp.where(inside_of(place), ordered[:, None], 0.0), axis=0)
    scores = rewards[0] - KL_WEIGHT * divergence
    same_prompt = prompt_index[0][:, None] == prompt_index[0][None, :]
    others = jnp.sum(jnp.where(same_prompt, scores[None, :], 0.0), axis=1) - scores
    advantage = scores - others / (K - 1)
    weight = jnp.sum(jnp.where(inside_of(row_place), advantage[None, :], 0.0), axis=1)

    weighted = (hidden.astype(jnp.float32) * weight[:, None]).astype(jnp.bfloat16)
    rows_first = (((0,), (0,)), ((), ()))
    grad_down = lax.dot_general(
        weighted, slopes_all, rows_first, preferred_element_type=jnp.float32
    )
    grad_hidden = weight[:, None] * lax.dot_general(
        slopes_all, pol_down_w, (((1,), (1,)), ((), ())), preferred_element_type=jnp.float32
    )
    sigmoid_gate = jax.nn.sigmoid(gate_pre)
    grad_gate_pre = grad_hidden * up_pre * sigmoid_gate * (1.0 + gate_pre * (1.0 - sigmoid_gate))
    grad_up_pre = grad_hidden * gate_pre * sigmoid_gate
    grad_gate = lax.dot_general(
        normed, grad_gate_pre.astype(jnp.bfloat16), rows_first, preferred_element_type=jnp.float32
    )
    grad_up = lax.dot_general(
        normed, grad_up_pre.astype(jnp.bfloat16), rows_first, preferred_element_type=jnp.float32
    )
    return grad_gate, grad_up, grad_down, advantage[None, :]


def combined_all(part, axis, combine):
    gathered = jax.tree.map(lambda a: lax.all_gather(a, axis), part)

    def take(source):
        return jax.tree.map(lambda a: lax.dynamic_index_in_dim(a, source, 0, False), gathered)

    return lax.fori_loop(
        1, lax.axis_size(axis), lambda source, state: combine(state, take(source)), take(0)
    )


def normalize(states, norm_gain):
    values = states.astype(jnp.float32)
    factor = lax.rsqrt(jnp.mean(values * values, axis=-1, keepdims=True) + EPSILON)
    return (values * factor * norm_gain).astype(jnp.bfloat16)


def combine_totals(first, second):
    row_peak = jnp.maximum(first[0], second[0])
    summed = first[1] * jnp.exp(first[0] - row_peak) + second[1] * jnp.exp(second[0] - row_peak)
    return (row_peak, summed, first[2] + second[2])


def column_section(normed_cols, state_cols, ids_all, weight_sets, group_index):
    col_width = state_cols.shape[1]
    unit_count = weight_sets[0][0].shape[1]
    in_weights = jnp.concatenate(
        [matrix for triple in weight_sets for matrix in triple[:2]], axis=1
    )
    row_block = normed_cols
    pre_sums = lax.psum_scatter(
        jnp.dot(row_block, in_weights, preferred_element_type=jnp.float32),
        "dp",
        scatter_dimension=0,
        tiled=True,
    )
    gate_pre = pre_sums[:, 0:unit_count]
    up_pre = pre_sums[:, unit_count : 2 * unit_count]
    activations = jax.nn.silu(gate_pre) * up_pre
    hidden_local = activations.astype(jnp.bfloat16)
    hidden_all = lax.all_gather(hidden_local, "dp", axis=0, tiled=True)
    row_block = hidden_all
    pieces = jnp.dot(row_block, weight_sets[0][2], preferred_element_type=jnp.float32)
    out_cols = lax.psum_scatter(pieces, "fsdp", scatter_dimension=0, tiled=True)
    states = state_cols.astype(jnp.float32)
    col_ids = jnp.arange(col_width, dtype=jnp.int32) + group_index * col_width
    logits = states + out_cols
    row_peak = jnp.max(logits, axis=1)
    logits_list = [logits]
    peaks = [row_peak]
    sums = [jnp.sum(jnp.exp(logits - row_peak[:, None]), axis=1)]
    picks = [jnp.sum(jnp.where(col_ids[None, :] == ids_all[:, None], logits, 0.0), axis=1)]
    row_peak, summed, picked = combined_all(
        (jnp.stack(peaks, axis=1), jnp.stack(sums, axis=1), jnp.stack(picks, axis=1)),
        "dp",
        combine_totals,
    )
    log_total = row_peak + jnp.log(summed)
    return (pre_sums, hidden_all, logits_list, log_total, picked - log_total)


def leave_one_out(log_gap, inside, prompt_index, rewards):
    divergence = lax.psum(jnp.sum(log_gap[:, None] * inside, axis=0), "fsdp")
    scores = rewards[0] - KL_WEIGHT * divergence
    same_prompt = (prompt_index[0][:, None] == prompt_index[0][None, :]).astype(jnp.float32)
    others = jnp.sum(same_prompt * scores[None, :], axis=1) - scores
    advantage = scores - others / (K - 1)
    weight = jnp.sum(inside * advantage[None, :], axis=1)
    return (advantage, weight)


def local(
    hidden_states,
    token_ids,
    norm_gain,
    ref_gate_w,
    ref_up_w,
    ref_down_w,
    pol_gate_w,
    pol_up_w,
    pol_down_w,
    sample_lengths,
    prompt_index,
    rewards,
):
    token_count = hidden_states.shape[0]
    model_width = hidden_states.shape[1]
    group_index = lax.axis_index("dp")
    member_index = lax.axis_index("fsdp")
    unit_count = pol_gate_w.shape[1]
    normed = normalize(hidden_states, norm_gain)
    normed_mixed, state_cols = (
        lax.all_to_all(normed, "dp", split_axis=1, concat_axis=0, tiled=True),
        lax.all_to_all(hidden_states, "dp", split_axis=1, concat_axis=0, tiled=True),
    )
    normed_cols = lax.all_gather(normed_mixed, "fsdp", axis=0, tiled=True)
    ids_all = lax.all_gather(token_ids, "dp", axis=0, tiled=True)
    own_start = group_index * token_count
    position = member_index * token_count + jnp.arange(token_count, dtype=jnp.int32)
    sample_ends = jnp.cumsum(sample_lengths[0])
    sample_starts = sample_ends - sample_lengths[0]
    inside = (
        (position[:, None] >= sample_starts[None, :]) & (position[:, None] < sample_ends[None, :])
    ).astype(jnp.float32)
    _, _, _, _, ref_lp = column_section(
        normed_cols, state_cols, ids_all, [(ref_gate_w, ref_up_w, ref_down_w)], group_index
    )
    ref_own = lax.dynamic_slice_in_dim(ref_lp[:, 0], own_start, token_count, 0)
    group_normed = lax.all_gather(normed, "fsdp", axis=0, tiled=True)
    row_block = group_normed
    gate_pre = jnp.dot(
        row_block,
        lax.all_gather(pol_gate_w, "dp", axis=0, tiled=True),
        preferred_element_type=jnp.float32,
    )
    up_pre = jnp.dot(
        row_block,
        lax.all_gather(pol_up_w, "dp", axis=0, tiled=True),
        preferred_element_type=jnp.float32,
    )
    down_full = lax.all_gather(pol_down_w, "dp", axis=1, tiled=True)
    hidden = (jax.nn.silu(gate_pre) * up_pre).astype(jnp.bfloat16)
    row_block = hidden
    pol_out = lax.psum_scatter(
        jnp.dot(row_block, down_full, preferred_element_type=jnp.float32),
        "fsdp",
        scatter_dimension=0,
        tiled=True,
    )
    logits = hidden_states.astype(jnp.float32) + pol_out
    row_peak = jnp.max(logits, axis=1)
    log_total = row_peak + jnp.log(jnp.sum(jnp.exp(logits - row_peak[:, None]), axis=1))
    columns = jnp.arange(model_width, dtype=jnp.int32)
    onehot = (columns[None, :] == token_ids[:, None]).astype(jnp.float32)
    pol_own = (
        jnp.sum(jnp.where(columns[None, :] == token_ids[:, None], logits, 0.0), axis=1) - log_total
    )
    advantage, weight = leave_one_out(pol_own - ref_own, inside, prompt_index, rewards)
    grad_logits = (-weight[:, None] * (onehot - jnp.exp(logits - log_total[:, None]))).astype(
        jnp.bfloat16
    )
    group_grads = lax.all_gather(grad_logits, "fsdp", axis=0, tiled=True)
    down_term = lax.dot_general(
        hidden, group_grads, (((0,), (0,)), ((), ())), preferred_element_type=jnp.float32
    )
    grad_down = lax.psum_scatter(
        down_term.astype(jnp.bfloat16), "dp", scatter_dimension=1, tiled=True
    ).astype(jnp.float32)
    grad_hidden = lax.dot_general(
        group_grads, down_full, (((1,), (1,)), ((), ())), preferred_element_type=jnp.float32
    )
    sigmoid_gate = jax.nn.sigmoid(gate_pre)
    grad_gate_pre = grad_hidden * up_pre * sigmoid_gate * (1.0 + gate_pre * (1.0 - sigmoid_gate))
    grad_up_pre = grad_hidden * gate_pre * sigmoid_gate
    gate_grads = jnp.concatenate(
        [grad_gate_pre.astype(jnp.bfloat16), grad_up_pre.astype(jnp.bfloat16)], axis=1
    )
    row_block = group_normed
    grad_inner = lax.psum_scatter(
        lax.dot_general(
            row_block, gate_grads, (((0,), (0,)), ((), ())), preferred_element_type=jnp.float32
        ).astype(jnp.bfloat16),
        "dp",
        scatter_dimension=0,
        tiled=True,
    ).astype(jnp.float32)
    return (grad_inner[:, :unit_count], grad_inner[:, unit_count:], grad_down, advantage[None, :])


def solution(mesh):
    members = mesh.shape["fsdp"]
    single = mesh.shape["dp"] == 1 and members > 1 and members & (members - 1) == 0
    return jax.shard_map(
        local_single if single else local,
        mesh=mesh,
        in_specs=(
            P(("dp", "fsdp"), None),
            P(("dp", "fsdp")),
            P(),
            P("dp", "fsdp"),
            P("dp", "fsdp"),
            P("fsdp", "dp"),
            P("dp", "fsdp"),
            P("dp", "fsdp"),
            P("fsdp", "dp"),
            P("dp", None),
            P("dp", None),
            P("dp", None),
        ),
        out_specs=(P("dp", "fsdp"), P("dp", "fsdp"), P("fsdp", "dp"), P("dp", None)),
        check_vma=False,
    )
```

```python
import functools

import jax
import jax.numpy as jnp
import numpy as np
from jax import lax
from jax.experimental import pallas as pl
from jax.experimental.pallas import tpu as pltpu
from jax.sharding import PartitionSpec as P

K = 8


EPSILON = 1e-06
KL_WEIGHT = 0.05
PIECES = 3
LANES = 128
FETCH_VMEM = 4 << 20
FORWARD_VMEM = 8 << 20
BACKWARD_VMEM = 36 << 20


def exchange_levels(members):
    bits = [1 << b for b in range(members.bit_length() - 1)]
    levels, rest = [bits[:1]], bits[1:]
    while rest:
        low, rest = rest[:2], rest[2:]
        levels.append(low + [low[0] | low[1]] if len(low) == 2 else low)
    return [level for level in levels if level]


def swap(values, mask):
    members = lax.axis_size("fsdp")
    return lax.ppermute(values, "fsdp", [(i, i ^ mask) for i in range(members)])


def tie(first, second):
    return lax.optimization_barrier((first, second))


def gather_blocks(rows, levels, beside=(None, None)):
    beside = list(beside)
    for level in reversed(levels[2:]):
        parts = [swap(rows, mask) for mask in level]
        if beside[0] is not None:
            parts, beside[0] = tie(parts, beside[0])
        rows = jnp.concatenate([rows] + parts, axis=0)
    blocks = [rows]
    if len(levels) > 1:
        blocks = blocks + [swap(rows, mask) for mask in levels[1]]
    if beside[1] is not None:
        blocks[1:], beside[1] = tie(blocks[1:], beside[1])
    return blocks + [swap(block, mask) for mask in levels[0] for block in blocks], beside


def scatter_rows(sums, levels):
    for level in levels:
        count = sums.shape[0] // (len(level) + 1)
        own = sums[:count]
        for place, mask in enumerate(level):
            block = sums[(place + 1) * count : (place + 2) * count]
            own = own + swap(block.astype(jnp.bfloat16), mask).astype(jnp.float32)
        sums = own
    return sums


def row_masks(levels):
    masks = np.zeros((1,), np.int32)
    for level in reversed(levels):
        masks = np.concatenate([masks] + [masks ^ mask for mask in level])
    return masks


def split_float(value):
    pieces = []
    for _ in range(PIECES):
        piece = lax.reduce_precision(value, 8, 7)
        pieces.append(piece)
        value = value - piece
    return pieces


NT = (((1,), (1,)), ((), ()))
NN = (((1,), (0,)), ((), ()))


def column_chunk(width):
    return 1024 if width % 1024 == 0 else width


def dot(left, right, dims):
    return lax.dot_general(left, right, dims, preferred_element_type=jnp.float32)


def fetch_kernel(*refs):
    count = len(refs) // 2
    sources, targets, sems = refs[:count], refs[count:-1], refs[-1]
    copies = [
        pltpu.make_async_copy(source, target, sems.at[place])
        for place, (source, target) in enumerate(zip(sources, targets))
    ]
    for copy in copies:
        copy.start()
    for copy in copies:
        copy.wait()


def fetch(weights):
    vmem = pl.BlockSpec(memory_space=pltpu.VMEM)
    hbm = pl.BlockSpec(memory_space=pltpu.HBM)
    return pl.pallas_call(
        fetch_kernel,
        out_shape=[jax.ShapeDtypeStruct(w.shape, w.dtype) for w in weights],
        in_specs=[hbm] * len(weights),
        out_specs=[vmem] * len(weights),
        scratch_shapes=[pltpu.SemaphoreType.DMA((len(weights),))],
        compiler_params=pltpu.CompilerParams(vmem_limit_bytes=FETCH_VMEM),
        cost_estimate=pl.CostEstimate(
            flops=0, bytes_accessed=sum(2 * w.size for w in weights), transcendentals=0
        ),
    )(*[pltpu.with_memory_space_constraint(w, pltpu.HBM) for w in weights])


def forward_model(weights, normed, hidden_rows, sent, kept, chunk):
    gate_w, up_w, down_w = weights
    half = kept.shape[0]
    gate = dot(gate_w[...], normed[...], NT)
    up = dot(up_w[...], normed[...], NT)
    hidden = gate * (1.0 / (1.0 + jnp.exp(-gate))) * up
    hidden_rows[...] = hidden.T.astype(jnp.bfloat16)

    def outer(step, _):
        columns = pl.ds(pl.multiple_of(step * chunk, chunk), chunk)
        part = dot(hidden_rows[...], down_w[:, columns], NN)
        kept[:, columns] = part[:half]
        sent[:, columns] = part[half:].astype(jnp.bfloat16)
        return 0

    lax.fori_loop(0, normed.shape[1] // chunk, outer, 0)
    return gate, up, hidden


def reference_kernel(block_count, chunk, *refs):
    blocks = refs[:block_count]
    gain, *weights = refs[block_count : block_count + 4]
    normed, sent, kept, hidden_rows = refs[block_count + 4 :]
    height = blocks[0].shape[0]
    for place, block in enumerate(blocks):
        values = block[...].astype(jnp.float32)
        factor = lax.rsqrt(jnp.mean(values * values, axis=1, keepdims=True) + EPSILON)
        normed[place * height : (place + 1) * height, :] = (values * factor * gain[...]).astype(
            jnp.bfloat16
        )
    forward_model(weights, normed, hidden_rows, sent, kept, chunk)


def policy_kernel(chunk, normed, *refs):
    weights = refs[:3]
    gate_out, up_out, hidden_out, sent, kept, hidden_rows = refs[3:]
    gate, up, hidden = forward_model(weights, normed, hidden_rows, sent, kept, chunk)
    gate_out[...] = gate
    up_out[...] = up
    hidden_out[...] = hidden.astype(jnp.bfloat16)


def forward_call(kernel, operands, extra, weights, tokens):
    units, width = weights[0].shape
    vmem = pl.BlockSpec(memory_space=pltpu.VMEM)
    shapes = extra + [
        jax.ShapeDtypeStruct((tokens // 2, width), jnp.bfloat16),
        jax.ShapeDtypeStruct((tokens // 2, width), jnp.float32),
    ]
    return pl.pallas_call(
        kernel,
        out_shape=shapes,
        in_specs=[vmem] * (len(operands) + 3),
        out_specs=[vmem] * len(shapes),
        scratch_shapes=[pltpu.VMEM((tokens, units), jnp.bfloat16)],
        compiler_params=pltpu.CompilerParams(vmem_limit_bytes=FORWARD_VMEM),
        cost_estimate=pl.CostEstimate(
            flops=6 * tokens * width * units,
            bytes_accessed=6 * units * width,
            transcendentals=tokens * units,
        ),
    )(*operands, *weights)


def forward_reference(blocks, gain, weights):
    width = blocks[0].shape[1]
    tokens = sum(block.shape[0] for block in blocks)
    return forward_call(
        functools.partial(reference_kernel, len(blocks), column_chunk(width)),
        blocks + [gain],
        [jax.ShapeDtypeStruct((tokens, width), jnp.bfloat16)],
        weights,
        tokens,
    )


def forward_policy(normed, weights):
    tokens, width = normed.shape
    units = weights[0].shape[0]
    return forward_call(
        functools.partial(policy_kernel, column_chunk(width)),
        [normed],
        [jax.ShapeDtypeStruct((units, tokens), jnp.float32)] * 2
        + [jax.ShapeDtypeStruct((units, tokens), jnp.bfloat16)],
        weights,
        tokens,
    )


def backward_kernel(block_count, chunk, *refs):
    blocks = refs[:block_count]
    normed, gate_ref, up_ref, hidden_ref, lengths, prompts, rewards, places, down = refs[
        block_count : block_count + 9
    ]
    grad_gate, grad_up, grad_down, advantage_out = refs[block_count + 9 : block_count + 13]
    slopes, held, total, gate_left, up_left, down_left, gate_buf, up_buf, down_buf, in_sems, sems = (
        refs[block_count + 13 :]
    )
    width = normed.shape[1]
    steps = width // chunk
    tokens = normed.shape[0]
    samples = lengths.shape[1]
    height = blocks[0].shape[0]

    def columns(step):
        return pl.ds(pl.multiple_of(step * chunk, chunk), chunk)

    def copy_in(step):
        return pltpu.make_async_copy(
            down.at[:, columns(step)], held.at[:, columns(step)], in_sems.at[step]
        )

    def copy_out(which, step):
        source = (gate_buf, up_buf, down_buf)[which]
        target = (grad_gate, grad_up, grad_down)[which]
        return pltpu.make_async_copy(
            source.at[:, columns(step)], target.at[:, columns(step)], sems.at[which, step]
        )

    for step in range(steps):
        copy_in(step).start()

    gaps = []
    for place, block in enumerate(blocks):
        slopes[place * height : (place + 1) * height, :] = block[:, :width]
        gaps.append(jnp.sum(block[:, width:].astype(jnp.float32), axis=1, keepdims=True))
    gap = jnp.concatenate(gaps, axis=0)

    row = lax.broadcasted_iota(jnp.int32, (samples, samples), 0)
    col = lax.broadcasted_iota(jnp.int32, (samples, samples), 1)
    diagonal = row == col

    def as_row(column):
        return jnp.sum(jnp.where(diagonal, column, 0.0), axis=0, keepdims=True)

    def as_column(line, mask):
        return jnp.sum(jnp.where(mask, line, 0.0), axis=1, keepdims=True)

    counts = lengths[...].astype(jnp.float32)
    ends = as_column(counts, col <= row)
    starts = ends - as_column(counts, diagonal)
    kinds = prompts[...].astype(jnp.float32)
    place_line = places[...].astype(jnp.float32)
    token_row = lax.broadcasted_iota(jnp.int32, (tokens, tokens), 0)
    token_col = lax.broadcasted_iota(jnp.int32, (tokens, tokens), 1)
    place_column = as_column(place_line, token_row == token_col)

    def inside(position):
        return (position >= starts) & (position < ends)

    lane = lax.broadcasted_iota(jnp.int32, (1, tokens), 1).astype(jnp.float32)
    ordered = jnp.sum(jnp.where(place_column == lane, gap, 0.0), axis=0, keepdims=True)
    divergence = as_column(ordered, inside(lane))
    scores = as_column(rewards[...], diagonal) - KL_WEIGHT * divergence
    others = as_column(as_row(scores), as_column(kinds, diagonal) == kinds) - scores
    advantage = scores - others / (K - 1)
    advantage_out[...] = as_row(advantage)
    weight = jnp.sum(jnp.where(inside(place_line), advantage, 0.0), axis=0, keepdims=True)

    down_left[...] = (hidden_ref[...].astype(jnp.float32) * weight).astype(jnp.bfloat16)
    total[...] = jnp.zeros_like(total)

    def first(step, _):
        down_buf[:, columns(step)] = dot(down_left[...], slopes[:, columns(step)], NN)
        copy_out(2, step).start()
        copy_in(step).wait()
        total[...] += dot(held[:, columns(step)], slopes[:, columns(step)], NT)
        return 0

    lax.fori_loop(0, steps, first, 0)
    grad_hidden = total[...] * weight
    gate = gate_ref[...]
    sigmoid = 1.0 / (1.0 + jnp.exp(-gate))
    gate_left[...] = (
        grad_hidden * up_ref[...] * sigmoid * (1.0 + gate * (1.0 - sigmoid))
    ).astype(jnp.bfloat16)
    up_left[...] = (grad_hidden * gate * sigmoid).astype(jnp.bfloat16)

    def second(step, _):
        for which, left, buffer in ((0, gate_left, gate_buf), (1, up_left, up_buf)):
            buffer[:, columns(step)] = dot(left[...], normed[:, columns(step)], NN)
            copy_out(which, step).start()
        return 0

    lax.fori_loop(0, steps, second, 0)

    def finish(step, _):
        for which in range(3):
            copy_out(which, step).wait()
        return 0

    lax.fori_loop(0, steps, finish, 0)


def backward(blocks, normed, gate, up, hidden, samples, down):
    tokens, width = normed.shape
    units = gate.shape[0]
    chunk = column_chunk(width)
    vmem = pl.BlockSpec(memory_space=pltpu.VMEM)
    hbm = pl.BlockSpec(memory_space=pl.ANY)
    grad = jax.ShapeDtypeStruct((units, width), jnp.float32)
    count = samples[0].shape[1]
    left = pltpu.VMEM((units, tokens), jnp.bfloat16)
    buffer = pltpu.VMEM((units, width), jnp.float32)
    steps = width // chunk
    return pl.pallas_call(
        functools.partial(backward_kernel, len(blocks), chunk),
        out_shape=(grad, grad, grad, jax.ShapeDtypeStruct((1, count), jnp.float32)),
        in_specs=[vmem] * (len(blocks) + 8) + [hbm],
        out_specs=(hbm, hbm, hbm, vmem),
        scratch_shapes=[
            pltpu.VMEM((tokens, width), jnp.bfloat16),
            pltpu.VMEM((units, width), jnp.bfloat16),
            pltpu.VMEM((units, tokens), jnp.float32),
            left,
            left,
            left,
            buffer,
            buffer,
            buffer,
            pltpu.SemaphoreType.DMA((steps,)),
            pltpu.SemaphoreType.DMA((3, steps)),
        ],
        compiler_params=pltpu.CompilerParams(vmem_limit_bytes=BACKWARD_VMEM),
        cost_estimate=pl.CostEstimate(
            flops=8 * tokens * width * units,
            bytes_accessed=14 * units * width,
            transcendentals=tokens * units,
        ),
    )(
        *blocks,
        normed,
        gate,
        up,
        hidden,
        *samples,
        pltpu.with_memory_space_constraint(down, pltpu.HBM),
    )


def local_single(
    hidden_states,
    token_ids,
    norm_gain,
    ref_gate_w,
    ref_up_w,
    ref_down_w,
    pol_gate_w,
    pol_up_w,
    pol_down_w,
    sample_lengths,
    prompt_index,
    rewards,
):
    token_count, width = hidden_states.shape
    levels = exchange_levels(lax.axis_size("fsdp"))
    masks = row_masks(levels)
    tokens = token_count * masks.size
    member = lax.axis_index("fsdp").astype(jnp.int32)

    blocks, (ref_weights, pol_weights) = gather_blocks(
        hidden_states,
        levels,
        (
            fetch([ref_gate_w.T, ref_up_w.T, ref_down_w]),
            fetch([pol_gate_w.T, pol_up_w.T, pol_down_w]),
        ),
    )
    normed, ref_sent, ref_kept = forward_reference(blocks, norm_gain[None, :], ref_weights)
    gate, up, hidden, pol_sent, pol_kept = forward_policy(normed, pol_weights)

    def reduce_rows(sent, kept):
        return scatter_rows(kept + swap(sent, levels[0][0]).astype(jnp.float32), levels[1:])

    ref_sums = reduce_rows(ref_sent, ref_kept)
    pol_sums = reduce_rows(pol_sent, pol_kept)

    states = hidden_states.astype(jnp.float32)
    columns = jnp.arange(width, dtype=jnp.int32)
    chosen = columns[None, :] == token_ids[:, None]

    def token_logprob(logits):
        row_peak = jnp.max(logits, axis=1)
        log_total = row_peak + jnp.log(jnp.sum(jnp.exp(logits - row_peak[:, None]), axis=1))
        return jnp.sum(jnp.where(chosen, logits, 0.0), axis=1) - log_total, log_total

    logits = states + pol_sums
    pol_lp, log_total = token_logprob(logits)
    ref_lp, _ = token_logprob(states + ref_sums)
    slopes = jnp.exp(logits - log_total[:, None]) - chosen.astype(jnp.float32)
    extra = jnp.stack(split_float(pol_lp - ref_lp), axis=1)
    extra = jnp.pad(extra, ((0, 0), (0, LANES - PIECES)))
    payload = jnp.concatenate([slopes, extra], axis=1).astype(jnp.bfloat16)

    row_place = (
        (member ^ jnp.asarray(np.repeat(masks, token_count))) * token_count
        + jnp.asarray(np.tile(np.arange(token_count, dtype=np.int32), masks.size))
    )
    slope_blocks, _ = gather_blocks(payload, levels)
    grad_gate, grad_up, grad_down, advantage = backward(
        slope_blocks,
        normed,
        gate,
        up,
        hidden,
        (sample_lengths, prompt_index, rewards, row_place[None, :]),
        pol_down_w,
    )
    return grad_gate.T, grad_up.T, grad_down, advantage


def combined_all(part, axis, combine):
    gathered = jax.tree.map(lambda a: lax.all_gather(a, axis), part)

    def take(source):
        return jax.tree.map(lambda a: lax.dynamic_index_in_dim(a, source, 0, False), gathered)

    return lax.fori_loop(
        1, lax.axis_size(axis), lambda source, state: combine(state, take(source)), take(0)
    )


def normalize(states, norm_gain):
    values = states.astype(jnp.float32)
    factor = lax.rsqrt(jnp.mean(values * values, axis=-1, keepdims=True) + EPSILON)
    return (values * factor * norm_gain).astype(jnp.bfloat16)


def combine_totals(first, second):
    row_peak = jnp.maximum(first[0], second[0])
    summed = first[1] * jnp.exp(first[0] - row_peak) + second[1] * jnp.exp(second[0] - row_peak)
    return (row_peak, summed, first[2] + second[2])


def column_section(normed_cols, state_cols, ids_all, weight_sets, group_index):
    col_width = state_cols.shape[1]
    unit_count = weight_sets[0][0].shape[1]
    in_weights = jnp.concatenate(
        [matrix for triple in weight_sets for matrix in triple[:2]], axis=1
    )
    row_block = normed_cols
    pre_sums = lax.psum_scatter(
        jnp.dot(row_block, in_weights, preferred_element_type=jnp.float32),
        "dp",
        scatter_dimension=0,
        tiled=True,
    )
    gate_pre = pre_sums[:, 0:unit_count]
    up_pre = pre_sums[:, unit_count : 2 * unit_count]
    activations = jax.nn.silu(gate_pre) * up_pre
    hidden_local = activations.astype(jnp.bfloat16)
    hidden_all = lax.all_gather(hidden_local, "dp", axis=0, tiled=True)
    row_block = hidden_all
    pieces = jnp.dot(row_block, weight_sets[0][2], preferred_element_type=jnp.float32)
    out_cols = lax.psum_scatter(pieces, "fsdp", scatter_dimension=0, tiled=True)
    states = state_cols.astype(jnp.float32)
    col_ids = jnp.arange(col_width, dtype=jnp.int32) + group_index * col_width
    logits = states + out_cols
    row_peak = jnp.max(logits, axis=1)
    logits_list = [logits]
    peaks = [row_peak]
    sums = [jnp.sum(jnp.exp(logits - row_peak[:, None]), axis=1)]
    picks = [jnp.sum(jnp.where(col_ids[None, :] == ids_all[:, None], logits, 0.0), axis=1)]
    row_peak, summed, picked = combined_all(
        (jnp.stack(peaks, axis=1), jnp.stack(sums, axis=1), jnp.stack(picks, axis=1)),
        "dp",
        combine_totals,
    )
    log_total = row_peak + jnp.log(summed)
    return (pre_sums, hidden_all, logits_list, log_total, picked - log_total)


def leave_one_out(log_gap, inside, prompt_index, rewards):
    divergence = lax.psum(jnp.sum(log_gap[:, None] * inside, axis=0), "fsdp")
    scores = rewards[0] - KL_WEIGHT * divergence
    same_prompt = (prompt_index[0][:, None] == prompt_index[0][None, :]).astype(jnp.float32)
    others = jnp.sum(same_prompt * scores[None, :], axis=1) - scores
    advantage = scores - others / (K - 1)
    weight = jnp.sum(inside * advantage[None, :], axis=1)
    return (advantage, weight)


def local(
    hidden_states,
    token_ids,
    norm_gain,
    ref_gate_w,
    ref_up_w,
    ref_down_w,
    pol_gate_w,
    pol_up_w,
    pol_down_w,
    sample_lengths,
    prompt_index,
    rewards,
):
    token_count = hidden_states.shape[0]
    model_width = hidden_states.shape[1]
    group_index = lax.axis_index("dp")
    member_index = lax.axis_index("fsdp")
    unit_count = pol_gate_w.shape[1]
    normed = normalize(hidden_states, norm_gain)
    normed_mixed, state_cols = (
        lax.all_to_all(normed, "dp", split_axis=1, concat_axis=0, tiled=True),
        lax.all_to_all(hidden_states, "dp", split_axis=1, concat_axis=0, tiled=True),
    )
    normed_cols = lax.all_gather(normed_mixed, "fsdp", axis=0, tiled=True)
    ids_all = lax.all_gather(token_ids, "dp", axis=0, tiled=True)
    own_start = group_index * token_count
    position = member_index * token_count + jnp.arange(token_count, dtype=jnp.int32)
    sample_ends = jnp.cumsum(sample_lengths[0])
    sample_starts = sample_ends - sample_lengths[0]
    inside = (
        (position[:, None] >= sample_starts[None, :]) & (position[:, None] < sample_ends[None, :])
    ).astype(jnp.float32)
    _, _, _, _, ref_lp = column_section(
        normed_cols, state_cols, ids_all, [(ref_gate_w, ref_up_w, ref_down_w)], group_index
    )
    ref_own = lax.dynamic_slice_in_dim(ref_lp[:, 0], own_start, token_count, 0)
    group_normed = lax.all_gather(normed, "fsdp", axis=0, tiled=True)
    row_block = group_normed
    gate_pre = jnp.dot(
        row_block,
        lax.all_gather(pol_gate_w, "dp", axis=0, tiled=True),
        preferred_element_type=jnp.float32,
    )
    up_pre = jnp.dot(
        row_block,
        lax.all_gather(pol_up_w, "dp", axis=0, tiled=True),
        preferred_element_type=jnp.float32,
    )
    down_full = lax.all_gather(pol_down_w, "dp", axis=1, tiled=True)
    hidden = (jax.nn.silu(gate_pre) * up_pre).astype(jnp.bfloat16)
    row_block = hidden
    pol_out = lax.psum_scatter(
        jnp.dot(row_block, down_full, preferred_element_type=jnp.float32),
        "fsdp",
        scatter_dimension=0,
        tiled=True,
    )
    logits = hidden_states.astype(jnp.float32) + pol_out
    row_peak = jnp.max(logits, axis=1)
    log_total = row_peak + jnp.log(jnp.sum(jnp.exp(logits - row_peak[:, None]), axis=1))
    columns = jnp.arange(model_width, dtype=jnp.int32)
    onehot = (columns[None, :] == token_ids[:, None]).astype(jnp.float32)
    pol_own = (
        jnp.sum(jnp.where(columns[None, :] == token_ids[:, None], logits, 0.0), axis=1) - log_total
    )
    advantage, weight = leave_one_out(pol_own - ref_own, inside, prompt_index, rewards)
    grad_logits = (-weight[:, None] * (onehot - jnp.exp(logits - log_total[:, None]))).astype(
        jnp.bfloat16
    )
    group_grads = lax.all_gather(grad_logits, "fsdp", axis=0, tiled=True)
    down_term = lax.dot_general(
        hidden, group_grads, (((0,), (0,)), ((), ())), preferred_element_type=jnp.float32
    )
    grad_down = lax.psum_scatter(
        down_term.astype(jnp.bfloat16), "dp", scatter_dimension=1, tiled=True
    ).astype(jnp.float32)
    grad_hidden = lax.dot_general(
        group_grads, down_full, (((1,), (1,)), ((), ())), preferred_element_type=jnp.float32
    )
    sigmoid_gate = jax.nn.sigmoid(gate_pre)
    grad_gate_pre = grad_hidden * up_pre * sigmoid_gate * (1.0 + gate_pre * (1.0 - sigmoid_gate))
    grad_up_pre = grad_hidden * gate_pre * sigmoid_gate
    gate_grads = jnp.concatenate(
        [grad_gate_pre.astype(jnp.bfloat16), grad_up_pre.astype(jnp.bfloat16)], axis=1
    )
    row_block = group_normed
    grad_inner = lax.psum_scatter(
        lax.dot_general(
            row_block, gate_grads, (((0,), (0,)), ((), ())), preferred_element_type=jnp.float32
        ).astype(jnp.bfloat16),
        "dp",
        scatter_dimension=0,
        tiled=True,
    ).astype(jnp.float32)
    return (grad_inner[:, :unit_count], grad_inner[:, unit_count:], grad_down, advantage[None, :])


def solution(mesh):
    members = mesh.shape["fsdp"]
    single = mesh.shape["dp"] == 1 and members > 1 and members & (members - 1) == 0
    return jax.shard_map(
        local_single if single else local,
        mesh=mesh,
        in_specs=(
            P(("dp", "fsdp"), None),
            P(("dp", "fsdp")),
            P(),
            P("dp", "fsdp"),
            P("dp", "fsdp"),
            P("fsdp", "dp"),
            P("dp", "fsdp"),
            P("dp", "fsdp"),
            P("fsdp", "dp"),
            P("dp", None),
            P("dp", None),
            P("dp", None),
        ),
        out_specs=(P("dp", "fsdp"), P("dp", "fsdp"), P("fsdp", "dp"), P("dp", None)),
        check_vma=False,
    )
```

```python
import functools

import jax
import jax.numpy as jnp
import numpy as np
from jax import lax
from jax.experimental import pallas as pl
from jax.experimental.pallas import tpu as pltpu
from jax.sharding import PartitionSpec as P

K = 8


EPSILON = 1e-06
KL_WEIGHT = 0.05
PIECES = 3
LANES = 128
FETCH_VMEM = 4 << 20
FORWARD_VMEM = 8 << 20
BACKWARD_VMEM = 32 << 20
BACKWARD_CHUNK = 1024


def exchange_levels(members):
    bits = [1 << b for b in range(members.bit_length() - 1)]
    levels, rest = [bits[:1]], bits[1:]
    while rest:
        low, rest = rest[:2], rest[2:]
        levels.append([low[0] | low[1], low[1], low[0]] if len(low) == 2 else low)
    return [level for level in levels if level]


def swap(values, mask):
    members = lax.axis_size("fsdp")
    return lax.ppermute(values, "fsdp", [(i, i ^ mask) for i in range(members)])


def tie(first, second):
    return lax.optimization_barrier((first, second))


def gather_blocks(rows, levels, beside=(None, None)):
    beside = list(beside)
    for level in reversed(levels[2:]):
        parts = [swap(rows, mask) for mask in level]
        if beside[0] is not None:
            parts, beside[0] = tie(parts, beside[0])
        rows = jnp.concatenate([rows] + parts, axis=0)
    blocks = [rows]
    if len(levels) > 1:
        blocks = blocks + [swap(rows, mask) for mask in levels[1]]
    if beside[1] is not None:
        blocks[1:], beside[1] = tie(blocks[1:], beside[1])
    return blocks + [swap(block, mask) for mask in levels[0] for block in blocks], beside


def scatter_rows(sums, levels):
    for level in levels:
        count = sums.shape[0] // (len(level) + 1)
        own = sums[:count]
        for place, mask in enumerate(level):
            block = sums[(place + 1) * count : (place + 2) * count]
            own = own + swap(block.astype(jnp.bfloat16), mask).astype(jnp.float32)
        sums = own
    return sums


def row_masks(levels):
    masks = np.zeros((1,), np.int32)
    for level in reversed(levels):
        masks = np.concatenate([masks] + [masks ^ mask for mask in level])
    return masks


def split_float(value):
    pieces = []
    for _ in range(PIECES):
        piece = lax.reduce_precision(value, 8, 7)
        pieces.append(piece)
        value = value - piece
    return pieces


NT = (((1,), (1,)), ((), ()))
NN = (((1,), (0,)), ((), ()))


def column_chunk(width, wanted=1024):
    return wanted if width % wanted == 0 else width


def dot(left, right, dims):
    return lax.dot_general(left, right, dims, preferred_element_type=jnp.float32)


def keep_in_hbm(array):
    return pltpu.with_memory_space_constraint(array, pltpu.HBM)


def fetch_kernel(*refs):
    count = len(refs) // 2
    sources, targets, sems = refs[:count], refs[count:-1], refs[-1]
    copies = [
        pltpu.make_async_copy(source, target, sems.at[place])
        for place, (source, target) in enumerate(zip(sources, targets))
    ]
    for copy in copies:
        copy.start()
    for copy in copies:
        copy.wait()


def fetch(weights):
    vmem = pl.BlockSpec(memory_space=pltpu.VMEM)
    hbm = pl.BlockSpec(memory_space=pltpu.HBM)
    return pl.pallas_call(
        fetch_kernel,
        out_shape=[jax.ShapeDtypeStruct(w.shape, w.dtype) for w in weights],
        in_specs=[hbm] * len(weights),
        out_specs=[vmem] * len(weights),
        scratch_shapes=[pltpu.SemaphoreType.DMA((len(weights),))],
        compiler_params=pltpu.CompilerParams(vmem_limit_bytes=FETCH_VMEM),
        cost_estimate=pl.CostEstimate(
            flops=0, bytes_accessed=sum(2 * w.size for w in weights), transcendentals=0
        ),
    )(*[keep_in_hbm(w) for w in weights])


def forward_model(weights, normed, hidden_rows, sent, kept, chunk):
    gate_w, up_w, down_w = weights
    half = kept.shape[0]
    gate = dot(gate_w[...], normed[...], NT)
    up = dot(up_w[...], normed[...], NT)
    hidden = gate * (1.0 / (1.0 + jnp.exp(-gate))) * up
    hidden_rows[...] = hidden.T.astype(jnp.bfloat16)

    def outer(step, _):
        columns = pl.ds(pl.multiple_of(step * chunk, chunk), chunk)
        part = dot(hidden_rows[...], down_w[:, columns], NN)
        kept[:, columns] = part[:half]
        sent[:, columns] = part[half:].astype(jnp.bfloat16)
        return 0

    lax.fori_loop(0, normed.shape[1] // chunk, outer, 0)
    return gate, up, hidden


def reference_kernel(block_count, chunk, *refs):
    blocks = refs[:block_count]
    gain, *weights = refs[block_count : block_count + 4]
    normed, sent, kept, hidden_rows = refs[block_count + 4 :]
    height = blocks[0].shape[0]
    for place, block in enumerate(blocks):
        values = block[...].astype(jnp.float32)
        factor = lax.rsqrt(jnp.mean(values * values, axis=1, keepdims=True) + EPSILON)
        normed[place * height : (place + 1) * height, :] = (values * factor * gain[...]).astype(
            jnp.bfloat16
        )
    forward_model(weights, normed, hidden_rows, sent, kept, chunk)


def policy_kernel(chunk, normed, *refs):
    weights = refs[:3]
    gate_out, up_out, hidden_out, sent, kept, hidden_rows = refs[3:]
    gate, up, hidden = forward_model(weights, normed, hidden_rows, sent, kept, chunk)
    gate_out[...] = gate
    up_out[...] = up
    hidden_out[...] = hidden.astype(jnp.bfloat16)


def forward_call(kernel, operands, extra, weights, tokens):
    units, width = weights[0].shape
    vmem = pl.BlockSpec(memory_space=pltpu.VMEM)
    shapes = extra + [
        jax.ShapeDtypeStruct((tokens // 2, width), jnp.bfloat16),
        jax.ShapeDtypeStruct((tokens // 2, width), jnp.float32),
    ]
    return pl.pallas_call(
        kernel,
        out_shape=shapes,
        in_specs=[vmem] * (len(operands) + 3),
        out_specs=[vmem] * len(shapes),
        scratch_shapes=[pltpu.VMEM((tokens, units), jnp.bfloat16)],
        compiler_params=pltpu.CompilerParams(vmem_limit_bytes=FORWARD_VMEM),
        cost_estimate=pl.CostEstimate(
            flops=6 * tokens * width * units,
            bytes_accessed=6 * units * width,
            transcendentals=tokens * units,
        ),
    )(*operands, *weights)


def forward_reference(blocks, gain, weights):
    width = blocks[0].shape[1]
    tokens = sum(block.shape[0] for block in blocks)
    return forward_call(
        functools.partial(reference_kernel, len(blocks), column_chunk(width)),
        blocks + [gain],
        [jax.ShapeDtypeStruct((tokens, width), jnp.bfloat16)],
        weights,
        tokens,
    )


def forward_policy(normed, weights):
    tokens, width = normed.shape
    units = weights[0].shape[0]
    return forward_call(
        functools.partial(policy_kernel, column_chunk(width)),
        [normed],
        [jax.ShapeDtypeStruct((units, tokens), jnp.float32)] * 2
        + [jax.ShapeDtypeStruct((units, tokens), jnp.bfloat16)],
        weights,
        tokens,
    )


def backward_kernel(block_count, chunk, token_count, *refs):
    blocks = refs[:block_count]
    normed, gate_ref, up_ref, hidden_ref, lengths, prompts, rewards, masks, down = refs[
        block_count : block_count + 9
    ]
    grad_gate, grad_up, grad_down, advantage_out = refs[block_count + 9 : block_count + 13]
    slopes, gate_left, up_left, down_left, gate_buf, up_buf, down_buf, sems = refs[
        block_count + 13 :
    ]
    width = normed.shape[1]
    steps = width // chunk
    tokens = normed.shape[0]
    samples = lengths.shape[1]
    height = blocks[0].shape[0]

    def columns(step):
        return pl.ds(pl.multiple_of(step * chunk, chunk), chunk)

    def copy_out(which, step):
        source = (gate_buf, up_buf, down_buf)[which]
        target = (grad_gate, grad_up, grad_down)[which]
        return pltpu.make_async_copy(
            source.at[:, columns(step)], target.at[:, columns(step)], sems.at[which, step]
        )

    gaps = []
    for place, block in enumerate(blocks):
        slopes[place * height : (place + 1) * height, :] = block[:, :width]
        gaps.append(jnp.sum(block[:, width:].astype(jnp.float32), axis=1, keepdims=True))
    gap = jnp.concatenate(gaps, axis=0)

    row = lax.broadcasted_iota(jnp.int32, (samples, samples), 0)
    col = lax.broadcasted_iota(jnp.int32, (samples, samples), 1)
    diagonal = row == col

    def as_row(column):
        return jnp.sum(jnp.where(diagonal, column, 0.0), axis=0, keepdims=True)

    def as_column(line, mask):
        return jnp.sum(jnp.where(mask, line, 0.0), axis=1, keepdims=True)

    counts = lengths[...].astype(jnp.float32)
    ends = as_column(counts, col <= row)
    starts = ends - as_column(counts, diagonal)
    kinds = prompts[...].astype(jnp.float32)
    own = lax.axis_index("fsdp").astype(jnp.int32)
    within = lax.broadcasted_iota(jnp.int32, (1, tokens), 1) % token_count
    place_line = ((masks[...] ^ own) * token_count + within).astype(jnp.float32)
    token_row = lax.broadcasted_iota(jnp.int32, (tokens, tokens), 0)
    token_col = lax.broadcasted_iota(jnp.int32, (tokens, tokens), 1)
    place_column = as_column(place_line, token_row == token_col)

    def inside(position):
        return (position >= starts) & (position < ends)

    lane = lax.broadcasted_iota(jnp.int32, (1, tokens), 1).astype(jnp.float32)
    ordered = jnp.sum(jnp.where(place_column == lane, gap, 0.0), axis=0, keepdims=True)
    divergence = as_column(ordered, inside(lane))
    scores = as_column(rewards[...], diagonal) - KL_WEIGHT * divergence
    others = as_column(as_row(scores), as_column(kinds, diagonal) == kinds) - scores
    advantage = scores - others / (K - 1)
    advantage_out[...] = as_row(advantage)
    weight = jnp.sum(jnp.where(inside(place_line), advantage, 0.0), axis=0, keepdims=True)

    down_left[...] = (hidden_ref[...].astype(jnp.float32) * weight).astype(jnp.bfloat16)

    def product(which, left, right, buffer):
        def body(step, _):
            buffer[:, columns(step)] = dot(left[...], right[:, columns(step)], NN)
            copy_out(which, step).start()
            return 0

        return body

    early = steps - steps // 4
    down_step = product(2, down_left, slopes, down_buf)
    lax.fori_loop(0, early, down_step, 0)
    grad_hidden = dot(down[...], slopes[...], NT) * weight
    lax.fori_loop(early, steps, down_step, 0)
    gate = gate_ref[...]
    sigmoid = 1.0 / (1.0 + jnp.exp(-gate))
    gate_left[...] = (
        grad_hidden * up_ref[...] * sigmoid * (1.0 + gate * (1.0 - sigmoid))
    ).astype(jnp.bfloat16)
    up_left[...] = (grad_hidden * gate * sigmoid).astype(jnp.bfloat16)
    lax.fori_loop(0, steps, product(0, gate_left, normed, gate_buf), 0)
    lax.fori_loop(0, steps, product(1, up_left, normed, up_buf), 0)

    def finish(step, _):
        for which in range(3):
            copy_out(which, step).wait()
        return 0

    lax.fori_loop(0, steps, finish, 0)


def backward(blocks, normed, gate, up, hidden, samples, down, token_count):
    tokens, width = normed.shape
    units = gate.shape[0]
    chunk = column_chunk(width, BACKWARD_CHUNK)
    vmem = pl.BlockSpec(memory_space=pltpu.VMEM)
    hbm = pl.BlockSpec(memory_space=pl.ANY)
    grad = jax.ShapeDtypeStruct((units, width), jnp.float32)
    count = samples[0].shape[1]
    left = pltpu.VMEM((units, tokens), jnp.bfloat16)
    buffer = pltpu.VMEM((units, width), jnp.float32)
    steps = width // chunk
    return pl.pallas_call(
        functools.partial(backward_kernel, len(blocks), chunk, token_count),
        out_shape=(grad, grad, grad, jax.ShapeDtypeStruct((1, count), jnp.float32)),
        in_specs=[vmem] * (len(blocks) + 9),
        out_specs=(hbm, hbm, hbm, vmem),
        scratch_shapes=[
            pltpu.VMEM((tokens, width), jnp.bfloat16),
            left,
            left,
            left,
            buffer,
            buffer,
            buffer,
            pltpu.SemaphoreType.DMA((3, steps)),
        ],
        compiler_params=pltpu.CompilerParams(vmem_limit_bytes=BACKWARD_VMEM),
        cost_estimate=pl.CostEstimate(
            flops=8 * tokens * width * units,
            bytes_accessed=14 * units * width,
            transcendentals=tokens * units,
        ),
    )(
        *blocks,
        normed,
        gate,
        up,
        hidden,
        *samples,
        down,
    )


def local_single(
    hidden_states,
    token_ids,
    norm_gain,
    ref_gate_w,
    ref_up_w,
    ref_down_w,
    pol_gate_w,
    pol_up_w,
    pol_down_w,
    sample_lengths,
    prompt_index,
    rewards,
):
    token_count, width = hidden_states.shape
    levels = exchange_levels(lax.axis_size("fsdp"))
    row_members = jnp.asarray(np.repeat(row_masks(levels), token_count))

    blocks, (ref_weights, pol_weights) = gather_blocks(
        hidden_states,
        levels,
        (
            fetch([ref_gate_w.T, ref_up_w.T, ref_down_w]),
            fetch([pol_gate_w.T, pol_up_w.T, pol_down_w]),
        ),
    )
    normed, ref_sent, ref_kept = forward_reference(blocks, norm_gain[None, :], ref_weights)
    gate, up, hidden, pol_sent, pol_kept = forward_policy(normed, pol_weights)

    def reduce_rows(sent, kept):
        return scatter_rows(kept + swap(sent, levels[0][0]).astype(jnp.float32), levels[1:])

    ref_sums = reduce_rows(ref_sent, ref_kept)
    pol_sums = reduce_rows(pol_sent, pol_kept)

    states = hidden_states.astype(jnp.float32)
    columns = jnp.arange(width, dtype=jnp.int32)
    chosen = columns[None, :] == token_ids[:, None]

    def token_logprob(logits):
        row_peak = jnp.max(logits, axis=1)
        log_total = row_peak + jnp.log(jnp.sum(jnp.exp(logits - row_peak[:, None]), axis=1))
        return jnp.sum(jnp.where(chosen, logits, 0.0), axis=1) - log_total, log_total

    logits = states + pol_sums
    pol_lp, log_total = token_logprob(logits)
    ref_lp, _ = token_logprob(states + ref_sums)
    slopes = jnp.exp(logits - log_total[:, None]) - chosen.astype(jnp.float32)
    extra = jnp.stack(split_float(pol_lp - ref_lp), axis=1)
    extra = jnp.pad(extra, ((0, 0), (0, LANES - PIECES)))
    payload = jnp.concatenate([slopes, extra], axis=1).astype(jnp.bfloat16)

    slope_blocks, (_, down_again) = gather_blocks(payload, levels, (None, fetch([pol_down_w])))
    grad_gate, grad_up, grad_down, advantage = backward(
        slope_blocks,
        normed,
        gate,
        up,
        hidden,
        (sample_lengths, prompt_index, rewards, row_members[None, :]),
        down_again[0],
        token_count,
    )
    return grad_gate.T, grad_up.T, grad_down, advantage


def combined_all(part, axis, combine):
    gathered = jax.tree.map(lambda a: lax.all_gather(a, axis), part)

    def take(source):
        return jax.tree.map(lambda a: lax.dynamic_index_in_dim(a, source, 0, False), gathered)

    return lax.fori_loop(
        1, lax.axis_size(axis), lambda source, state: combine(state, take(source)), take(0)
    )


def normalize(states, norm_gain):
    values = states.astype(jnp.float32)
    factor = lax.rsqrt(jnp.mean(values * values, axis=-1, keepdims=True) + EPSILON)
    return (values * factor * norm_gain).astype(jnp.bfloat16)


def combine_totals(first, second):
    row_peak = jnp.maximum(first[0], second[0])
    summed = first[1] * jnp.exp(first[0] - row_peak) + second[1] * jnp.exp(second[0] - row_peak)
    return (row_peak, summed, first[2] + second[2])


def column_section(normed_cols, state_cols, ids_all, weight_sets, group_index):
    col_width = state_cols.shape[1]
    unit_count = weight_sets[0][0].shape[1]
    in_weights = jnp.concatenate(
        [matrix for triple in weight_sets for matrix in triple[:2]], axis=1
    )
    row_block = normed_cols
    pre_sums = lax.psum_scatter(
        jnp.dot(row_block, in_weights, preferred_element_type=jnp.float32),
        "dp",
        scatter_dimension=0,
        tiled=True,
    )
    gate_pre = pre_sums[:, 0:unit_count]
    up_pre = pre_sums[:, unit_count : 2 * unit_count]
    activations = jax.nn.silu(gate_pre) * up_pre
    hidden_local = activations.astype(jnp.bfloat16)
    hidden_all = lax.all_gather(hidden_local, "dp", axis=0, tiled=True)
    row_block = hidden_all
    pieces = jnp.dot(row_block, weight_sets[0][2], preferred_element_type=jnp.float32)
    out_cols = lax.psum_scatter(pieces, "fsdp", scatter_dimension=0, tiled=True)
    states = state_cols.astype(jnp.float32)
    col_ids = jnp.arange(col_width, dtype=jnp.int32) + group_index * col_width
    logits = states + out_cols
    row_peak = jnp.max(logits, axis=1)
    logits_list = [logits]
    peaks = [row_peak]
    sums = [jnp.sum(jnp.exp(logits - row_peak[:, None]), axis=1)]
    picks = [jnp.sum(jnp.where(col_ids[None, :] == ids_all[:, None], logits, 0.0), axis=1)]
    row_peak, summed, picked = combined_all(
        (jnp.stack(peaks, axis=1), jnp.stack(sums, axis=1), jnp.stack(picks, axis=1)),
        "dp",
        combine_totals,
    )
    log_total = row_peak + jnp.log(summed)
    return (pre_sums, hidden_all, logits_list, log_total, picked - log_total)


def leave_one_out(log_gap, inside, prompt_index, rewards):
    divergence = lax.psum(jnp.sum(log_gap[:, None] * inside, axis=0), "fsdp")
    scores = rewards[0] - KL_WEIGHT * divergence
    same_prompt = (prompt_index[0][:, None] == prompt_index[0][None, :]).astype(jnp.float32)
    others = jnp.sum(same_prompt * scores[None, :], axis=1) - scores
    advantage = scores - others / (K - 1)
    weight = jnp.sum(inside * advantage[None, :], axis=1)
    return (advantage, weight)


def local(
    hidden_states,
    token_ids,
    norm_gain,
    ref_gate_w,
    ref_up_w,
    ref_down_w,
    pol_gate_w,
    pol_up_w,
    pol_down_w,
    sample_lengths,
    prompt_index,
    rewards,
):
    token_count = hidden_states.shape[0]
    model_width = hidden_states.shape[1]
    group_index = lax.axis_index("dp")
    member_index = lax.axis_index("fsdp")
    unit_count = pol_gate_w.shape[1]
    normed = normalize(hidden_states, norm_gain)
    normed_mixed, state_cols = (
        lax.all_to_all(normed, "dp", split_axis=1, concat_axis=0, tiled=True),
        lax.all_to_all(hidden_states, "dp", split_axis=1, concat_axis=0, tiled=True),
    )
    normed_cols = lax.all_gather(normed_mixed, "fsdp", axis=0, tiled=True)
    ids_all = lax.all_gather(token_ids, "dp", axis=0, tiled=True)
    own_start = group_index * token_count
    position = member_index * token_count + jnp.arange(token_count, dtype=jnp.int32)
    sample_ends = jnp.cumsum(sample_lengths[0])
    sample_starts = sample_ends - sample_lengths[0]
    inside = (
        (position[:, None] >= sample_starts[None, :]) & (position[:, None] < sample_ends[None, :])
    ).astype(jnp.float32)
    _, _, _, _, ref_lp = column_section(
        normed_cols, state_cols, ids_all, [(ref_gate_w, ref_up_w, ref_down_w)], group_index
    )
    ref_own = lax.dynamic_slice_in_dim(ref_lp[:, 0], own_start, token_count, 0)
    group_normed = lax.all_gather(normed, "fsdp", axis=0, tiled=True)
    row_block = group_normed
    gate_pre = jnp.dot(
        row_block,
        lax.all_gather(pol_gate_w, "dp", axis=0, tiled=True),
        preferred_element_type=jnp.float32,
    )
    up_pre = jnp.dot(
        row_block,
        lax.all_gather(pol_up_w, "dp", axis=0, tiled=True),
        preferred_element_type=jnp.float32,
    )
    down_full = lax.all_gather(pol_down_w, "dp", axis=1, tiled=True)
    hidden = (jax.nn.silu(gate_pre) * up_pre).astype(jnp.bfloat16)
    row_block = hidden
    pol_out = lax.psum_scatter(
        jnp.dot(row_block, down_full, preferred_element_type=jnp.float32),
        "fsdp",
        scatter_dimension=0,
        tiled=True,
    )
    logits = hidden_states.astype(jnp.float32) + pol_out
    row_peak = jnp.max(logits, axis=1)
    log_total = row_peak + jnp.log(jnp.sum(jnp.exp(logits - row_peak[:, None]), axis=1))
    columns = jnp.arange(model_width, dtype=jnp.int32)
    onehot = (columns[None, :] == token_ids[:, None]).astype(jnp.float32)
    pol_own = (
        jnp.sum(jnp.where(columns[None, :] == token_ids[:, None], logits, 0.0), axis=1) - log_total
    )
    advantage, weight = leave_one_out(pol_own - ref_own, inside, prompt_index, rewards)
    grad_logits = (-weight[:, None] * (onehot - jnp.exp(logits - log_total[:, None]))).astype(
        jnp.bfloat16
    )
    group_grads = lax.all_gather(grad_logits, "fsdp", axis=0, tiled=True)
    down_term = lax.dot_general(
        hidden, group_grads, (((0,), (0,)), ((), ())), preferred_element_type=jnp.float32
    )
    grad_down = lax.psum_scatter(
        down_term.astype(jnp.bfloat16), "dp", scatter_dimension=1, tiled=True
    ).astype(jnp.float32)
    grad_hidden = lax.dot_general(
        group_grads, down_full, (((1,), (1,)), ((), ())), preferred_element_type=jnp.float32
    )
    sigmoid_gate = jax.nn.sigmoid(gate_pre)
    grad_gate_pre = grad_hidden * up_pre * sigmoid_gate * (1.0 + gate_pre * (1.0 - sigmoid_gate))
    grad_up_pre = grad_hidden * gate_pre * sigmoid_gate
    gate_grads = jnp.concatenate(
        [grad_gate_pre.astype(jnp.bfloat16), grad_up_pre.astype(jnp.bfloat16)], axis=1
    )
    row_block = group_normed
    grad_inner = lax.psum_scatter(
        lax.dot_general(
            row_block, gate_grads, (((0,), (0,)), ((), ())), preferred_element_type=jnp.float32
        ).astype(jnp.bfloat16),
        "dp",
        scatter_dimension=0,
        tiled=True,
    ).astype(jnp.float32)
    return (grad_inner[:, :unit_count], grad_inner[:, unit_count:], grad_down, advantage[None, :])


def solution(mesh):
    members = mesh.shape["fsdp"]
    single = mesh.shape["dp"] == 1 and members > 1 and members & (members - 1) == 0
    return jax.shard_map(
        local_single if single else local,
        mesh=mesh,
        in_specs=(
            P(("dp", "fsdp"), None),
            P(("dp", "fsdp")),
            P(),
            P("dp", "fsdp"),
            P("dp", "fsdp"),
            P("fsdp", "dp"),
            P("dp", "fsdp"),
            P("dp", "fsdp"),
            P("fsdp", "dp"),
            P("dp", None),
            P("dp", None),
            P("dp", None),
        ),
        out_specs=(P("dp", "fsdp"), P("dp", "fsdp"), P("fsdp", "dp"), P("dp", None)),
        check_vma=False,
    )
```

```python
import functools

import jax
import jax.numpy as jnp
import numpy as np
from jax import lax
from jax.experimental import pallas as pl
from jax.experimental.pallas import tpu as pltpu
from jax.sharding import PartitionSpec as P

K = 8


EPSILON = 1e-06
KL_WEIGHT = 0.05
PIECES = 3
LANES = 128
FETCH_VMEM = 4 << 20
FORWARD_VMEM = 8 << 20
BACKWARD_VMEM = 32 << 20
BACKWARD_CHUNK = 1024


def exchange_levels(members):
    bits = [1 << b for b in range(members.bit_length() - 1)]
    levels, rest = [bits[:1]], bits[1:]
    while rest:
        low, rest = rest[:2], rest[2:]
        levels.append([low[0] | low[1], low[1], low[0]] if len(low) == 2 else low)
    return [level for level in levels if level]


def swap(values, mask):
    members = lax.axis_size("fsdp")
    return lax.ppermute(values, "fsdp", [(i, i ^ mask) for i in range(members)])


def tie(first, second):
    return lax.optimization_barrier((first, second))


def gather_blocks(rows, levels, beside=(None, None)):
    beside = list(beside)
    for level in reversed(levels[2:]):
        parts = [swap(rows, mask) for mask in level]
        if beside[0] is not None:
            parts, beside[0] = tie(parts, beside[0])
        rows = jnp.concatenate([rows] + parts, axis=0)
    blocks = [rows]
    if len(levels) > 1:
        blocks = blocks + [swap(rows, mask) for mask in levels[1]]
    if beside[1] is not None:
        blocks[1], beside[1] = tie(blocks[1], beside[1])
    return blocks + [swap(block, mask) for mask in levels[0] for block in blocks], beside


def scatter_rows(sums, levels):
    received = []
    for level in levels:
        for part in received:
            sums = sums + part.astype(jnp.float32)
        count = sums.shape[0] // (len(level) + 1)
        blocks = sums[count:].astype(jnp.bfloat16)
        received = [
            swap(blocks[place * count : (place + 1) * count], mask)
            for place, mask in enumerate(level)
        ]
        sums = sums[:count]
    return [sums] + received


def row_masks(levels):
    masks = np.zeros((1,), np.int32)
    for level in reversed(levels):
        masks = np.concatenate([masks] + [masks ^ mask for mask in level])
    return masks


def slope_kernel(parts, *refs):
    pol_parts, ref_parts = refs[:parts], refs[parts : 2 * parts]
    states_ref, ids, payload = refs[2 * parts :]
    count, width = states_ref.shape
    states = states_ref[...].astype(jnp.float32)
    chosen = lax.broadcasted_iota(jnp.int32, (count, width), 1) == ids[...]

    def token_logprob(terms):
        logits = states
        for term in terms:
            logits = logits + term[...].astype(jnp.float32)
        row_peak = jnp.max(logits, axis=1, keepdims=True)
        total = jnp.sum(jnp.exp(logits - row_peak), axis=1, keepdims=True)
        log_total = row_peak + jnp.log(total)
        picked = jnp.sum(jnp.where(chosen, logits, 0.0), axis=1, keepdims=True)
        return logits, log_total, picked - log_total

    logits, log_total, pol_lp = token_logprob(pol_parts)
    _, _, ref_lp = token_logprob(ref_parts)
    slopes = jnp.exp(logits - log_total) - jnp.where(chosen, 1.0, 0.0)
    payload[:, :width] = slopes.astype(jnp.bfloat16)
    lane = lax.broadcasted_iota(jnp.int32, (count, LANES), 1)
    rest = pol_lp - ref_lp
    extra = jnp.zeros((count, LANES), jnp.float32)
    for place in range(PIECES):
        piece = rest.astype(jnp.bfloat16).astype(jnp.float32)
        extra = jnp.where(lane == place, piece, extra)
        rest = rest - piece
    payload[:, width:] = extra.astype(jnp.bfloat16)


def slope_rows(pol_parts, ref_parts, states, ids):
    count, width = states.shape
    vmem = pl.BlockSpec(memory_space=pltpu.VMEM)
    return pl.pallas_call(
        functools.partial(slope_kernel, len(pol_parts)),
        out_shape=jax.ShapeDtypeStruct((count, width + LANES), jnp.bfloat16),
        in_specs=[vmem] * (2 * len(pol_parts) + 2),
        out_specs=vmem,
        compiler_params=pltpu.CompilerParams(vmem_limit_bytes=FETCH_VMEM),
    )(*pol_parts, *ref_parts, states, ids)


NT = (((1,), (1,)), ((), ()))
NN = (((1,), (0,)), ((), ()))


def column_chunk(width, wanted=1024):
    return wanted if width % wanted == 0 else width


def dot(left, right, dims):
    return lax.dot_general(left, right, dims, preferred_element_type=jnp.float32)


def keep_in_hbm(array):
    return pltpu.with_memory_space_constraint(array, pltpu.HBM)


def fetch_kernel(*refs):
    count = len(refs) // 2
    sources, targets, sems = refs[:count], refs[count:-1], refs[-1]
    copies = [
        pltpu.make_async_copy(source, target, sems.at[place])
        for place, (source, target) in enumerate(zip(sources, targets))
    ]
    for copy in copies:
        copy.start()
    for copy in copies:
        copy.wait()


def fetch(weights):
    vmem = pl.BlockSpec(memory_space=pltpu.VMEM)
    hbm = pl.BlockSpec(memory_space=pltpu.HBM)
    return pl.pallas_call(
        fetch_kernel,
        out_shape=[jax.ShapeDtypeStruct(w.shape, w.dtype) for w in weights],
        in_specs=[hbm] * len(weights),
        out_specs=[vmem] * len(weights),
        scratch_shapes=[pltpu.SemaphoreType.DMA((len(weights),))],
        compiler_params=pltpu.CompilerParams(vmem_limit_bytes=FETCH_VMEM),
        cost_estimate=pl.CostEstimate(
            flops=0, bytes_accessed=sum(2 * w.size for w in weights), transcendentals=0
        ),
    )(*[keep_in_hbm(w) for w in weights])


def forward_model(weights, normed, hidden_rows, sent, kept, chunk):
    gate_w, up_w, down_w = weights
    half = kept.shape[0]
    gate = dot(gate_w[...], normed[...], NT)
    up = dot(up_w[...], normed[...], NT)
    hidden = gate * (1.0 / (1.0 + jnp.exp(-gate))) * up
    hidden_rows[...] = hidden.T.astype(jnp.bfloat16)

    def outer(step, _):
        columns = pl.ds(pl.multiple_of(step * chunk, chunk), chunk)
        part = dot(hidden_rows[...], down_w[:, columns], NN)
        kept[:, columns] = part[:half]
        sent[:, columns] = part[half:].astype(jnp.bfloat16)
        return 0

    lax.fori_loop(0, normed.shape[1] // chunk, outer, 0)
    return gate, up, hidden


def reference_kernel(block_count, chunk, *refs):
    blocks = refs[:block_count]
    gain, *weights = refs[block_count : block_count + 4]
    normed, sent, kept, hidden_rows = refs[block_count + 4 :]
    height = blocks[0].shape[0]
    for place, block in enumerate(blocks):
        values = block[...].astype(jnp.float32)
        factor = lax.rsqrt(jnp.mean(values * values, axis=1, keepdims=True) + EPSILON)
        normed[place * height : (place + 1) * height, :] = (values * factor * gain[...]).astype(
            jnp.bfloat16
        )
    forward_model(weights, normed, hidden_rows, sent, kept, chunk)


def policy_kernel(chunk, normed, *refs):
    weights = refs[:3]
    gate_out, up_out, hidden_out, sent, kept, hidden_rows = refs[3:]
    gate, up, hidden = forward_model(weights, normed, hidden_rows, sent, kept, chunk)
    gate_out[...] = gate
    up_out[...] = up
    hidden_out[...] = hidden.astype(jnp.bfloat16)


def forward_call(kernel, operands, extra, weights, tokens):
    units, width = weights[0].shape
    vmem = pl.BlockSpec(memory_space=pltpu.VMEM)
    shapes = extra + [
        jax.ShapeDtypeStruct((tokens // 2, width), jnp.bfloat16),
        jax.ShapeDtypeStruct((tokens // 2, width), jnp.float32),
    ]
    return pl.pallas_call(
        kernel,
        out_shape=shapes,
        in_specs=[vmem] * (len(operands) + 3),
        out_specs=[vmem] * len(shapes),
        scratch_shapes=[pltpu.VMEM((tokens, units), jnp.bfloat16)],
        compiler_params=pltpu.CompilerParams(vmem_limit_bytes=FORWARD_VMEM),
        cost_estimate=pl.CostEstimate(
            flops=6 * tokens * width * units,
            bytes_accessed=6 * units * width,
            transcendentals=tokens * units,
        ),
    )(*operands, *weights)


def forward_reference(blocks, gain, weights):
    width = blocks[0].shape[1]
    tokens = sum(block.shape[0] for block in blocks)
    return forward_call(
        functools.partial(reference_kernel, len(blocks), column_chunk(width)),
        blocks + [gain],
        [jax.ShapeDtypeStruct((tokens, width), jnp.bfloat16)],
        weights,
        tokens,
    )


def forward_policy(normed, weights):
    tokens, width = normed.shape
    units = weights[0].shape[0]
    return forward_call(
        functools.partial(policy_kernel, column_chunk(width)),
        [normed],
        [jax.ShapeDtypeStruct((units, tokens), jnp.float32)] * 2
        + [jax.ShapeDtypeStruct((units, tokens), jnp.bfloat16)],
        weights,
        tokens,
    )


def backward_kernel(block_count, chunk, token_count, *refs):
    blocks = refs[:block_count]
    normed, gate_ref, up_ref, hidden_ref, lengths, prompts, rewards, masks, down = refs[
        block_count : block_count + 9
    ]
    grad_gate, grad_up, grad_down, advantage_out = refs[block_count + 9 : block_count + 13]
    slopes, gate_left, up_left, down_left, gate_buf, up_buf, down_buf, sems = refs[
        block_count + 13 :
    ]
    width = normed.shape[1]
    steps = width // chunk
    tokens = normed.shape[0]
    samples = lengths.shape[1]
    height = blocks[0].shape[0]

    def columns(step):
        return pl.ds(pl.multiple_of(step * chunk, chunk), chunk)

    def copy_out(which, step):
        source = (gate_buf, up_buf, down_buf)[which]
        target = (grad_gate, grad_up, grad_down)[which]
        return pltpu.make_async_copy(
            source.at[:, columns(step)], target.at[:, columns(step)], sems.at[which, step]
        )

    gaps = []
    for place, block in enumerate(blocks):
        slopes[place * height : (place + 1) * height, :] = block[:, :width]
        gaps.append(jnp.sum(block[:, width:].astype(jnp.float32), axis=1, keepdims=True))
    gap = jnp.concatenate(gaps, axis=0)

    row = lax.broadcasted_iota(jnp.int32, (samples, samples), 0)
    col = lax.broadcasted_iota(jnp.int32, (samples, samples), 1)
    diagonal = row == col

    def as_row(column):
        return jnp.sum(jnp.where(diagonal, column, 0.0), axis=0, keepdims=True)

    def as_column(line, mask):
        return jnp.sum(jnp.where(mask, line, 0.0), axis=1, keepdims=True)

    counts = lengths[...].astype(jnp.float32)
    ends = as_column(counts, col <= row)
    starts = ends - as_column(counts, diagonal)
    kinds = prompts[...].astype(jnp.float32)
    own = lax.axis_index("fsdp").astype(jnp.int32)
    within = lax.broadcasted_iota(jnp.int32, (1, tokens), 1) % token_count
    place_line = ((masks[...] ^ own) * token_count + within).astype(jnp.float32)
    token_row = lax.broadcasted_iota(jnp.int32, (tokens, tokens), 0)
    token_col = lax.broadcasted_iota(jnp.int32, (tokens, tokens), 1)
    place_column = as_column(place_line, token_row == token_col)

    def inside(position):
        return (position >= starts) & (position < ends)

    lane = lax.broadcasted_iota(jnp.int32, (1, tokens), 1).astype(jnp.float32)
    ordered = jnp.sum(jnp.where(place_column == lane, gap, 0.0), axis=0, keepdims=True)
    divergence = as_column(ordered, inside(lane))
    scores = as_column(rewards[...], diagonal) - KL_WEIGHT * divergence
    others = as_column(as_row(scores), as_column(kinds, diagonal) == kinds) - scores
    advantage = scores - others / (K - 1)
    advantage_out[...] = as_row(advantage)
    weight = jnp.sum(jnp.where(inside(place_line), advantage, 0.0), axis=0, keepdims=True)

    down_left[...] = (hidden_ref[...].astype(jnp.float32) * weight).astype(jnp.bfloat16)

    def product(which, left, right, buffer):
        def body(step, _):
            buffer[:, columns(step)] = dot(left[...], right[:, columns(step)], NN)
            copy_out(which, step).start()
            return 0

        return body

    early = steps - steps // 4
    down_step = product(2, down_left, slopes, down_buf)
    lax.fori_loop(0, early, down_step, 0)
    grad_hidden = dot(down[...], slopes[...], NT) * weight
    lax.fori_loop(early, steps, down_step, 0)
    gate = gate_ref[...]
    sigmoid = 1.0 / (1.0 + jnp.exp(-gate))
    gate_left[...] = (
        grad_hidden * up_ref[...] * sigmoid * (1.0 + gate * (1.0 - sigmoid))
    ).astype(jnp.bfloat16)
    up_left[...] = (grad_hidden * gate * sigmoid).astype(jnp.bfloat16)
    lax.fori_loop(0, steps, product(0, gate_left, normed, gate_buf), 0)
    lax.fori_loop(0, steps, product(1, up_left, normed, up_buf), 0)

    def finish(step, _):
        for which in range(3):
            copy_out(which, step).wait()
        return 0

    lax.fori_loop(0, steps, finish, 0)


def backward(blocks, normed, gate, up, hidden, samples, down, token_count):
    tokens, width = normed.shape
    units = gate.shape[0]
    chunk = column_chunk(width, BACKWARD_CHUNK)
    vmem = pl.BlockSpec(memory_space=pltpu.VMEM)
    hbm = pl.BlockSpec(memory_space=pl.ANY)
    grad = jax.ShapeDtypeStruct((units, width), jnp.float32)
    count = samples[0].shape[1]
    left = pltpu.VMEM((units, tokens), jnp.bfloat16)
    buffer = pltpu.VMEM((units, width), jnp.float32)
    steps = width // chunk
    return pl.pallas_call(
        functools.partial(backward_kernel, len(blocks), chunk, token_count),
        out_shape=(grad, grad, grad, jax.ShapeDtypeStruct((1, count), jnp.float32)),
        in_specs=[vmem] * (len(blocks) + 9),
        out_specs=(hbm, hbm, hbm, vmem),
        scratch_shapes=[
            pltpu.VMEM((tokens, width), jnp.bfloat16),
            left,
            left,
            left,
            buffer,
            buffer,
            buffer,
            pltpu.SemaphoreType.DMA((3, steps)),
        ],
        compiler_params=pltpu.CompilerParams(vmem_limit_bytes=BACKWARD_VMEM),
        cost_estimate=pl.CostEstimate(
            flops=8 * tokens * width * units,
            bytes_accessed=14 * units * width,
            transcendentals=tokens * units,
        ),
    )(
        *blocks,
        normed,
        gate,
        up,
        hidden,
        *samples,
        down,
    )


def local_single(
    hidden_states,
    token_ids,
    norm_gain,
    ref_gate_w,
    ref_up_w,
    ref_down_w,
    pol_gate_w,
    pol_up_w,
    pol_down_w,
    sample_lengths,
    prompt_index,
    rewards,
):
    token_count, width = hidden_states.shape
    levels = exchange_levels(lax.axis_size("fsdp"))
    row_members = jnp.asarray(np.repeat(row_masks(levels), token_count))

    blocks, (ref_weights, pol_weights) = gather_blocks(
        hidden_states,
        levels,
        (
            fetch([ref_gate_w.T, ref_up_w.T, ref_down_w]),
            fetch([pol_gate_w.T, pol_up_w.T, pol_down_w]),
        ),
    )
    normed, ref_sent, ref_kept = forward_reference(blocks, norm_gain[None, :], ref_weights)
    gate, up, hidden, pol_sent, pol_kept = forward_policy(normed, pol_weights)

    def reduce_rows(sent, kept):
        return scatter_rows(kept + swap(sent, levels[0][0]).astype(jnp.float32), levels[1:])

    ref_parts = reduce_rows(ref_sent, ref_kept)
    pol_parts = reduce_rows(pol_sent, pol_kept)
    payload = slope_rows(pol_parts, ref_parts, hidden_states, token_ids[:, None])
    slope_blocks, (_, down_again) = gather_blocks(payload, levels, (None, fetch([pol_down_w])))
    grad_gate, grad_up, grad_down, advantage = backward(
        slope_blocks,
        normed,
        gate,
        up,
        hidden,
        (sample_lengths, prompt_index, rewards, row_members[None, :]),
        down_again[0],
        token_count,
    )
    return grad_gate.T, grad_up.T, grad_down, advantage


def combined_all(part, axis, combine):
    gathered = jax.tree.map(lambda a: lax.all_gather(a, axis), part)

    def take(source):
        return jax.tree.map(lambda a: lax.dynamic_index_in_dim(a, source, 0, False), gathered)

    return lax.fori_loop(
        1, lax.axis_size(axis), lambda source, state: combine(state, take(source)), take(0)
    )


def normalize(states, norm_gain):
    values = states.astype(jnp.float32)
    factor = lax.rsqrt(jnp.mean(values * values, axis=-1, keepdims=True) + EPSILON)
    return (values * factor * norm_gain).astype(jnp.bfloat16)


def combine_totals(first, second):
    row_peak = jnp.maximum(first[0], second[0])
    summed = first[1] * jnp.exp(first[0] - row_peak) + second[1] * jnp.exp(second[0] - row_peak)
    return (row_peak, summed, first[2] + second[2])


def column_section(normed_cols, state_cols, ids_all, weight_sets, group_index):
    col_width = state_cols.shape[1]
    unit_count = weight_sets[0][0].shape[1]
    in_weights = jnp.concatenate(
        [matrix for triple in weight_sets for matrix in triple[:2]], axis=1
    )
    row_block = normed_cols
    pre_sums = lax.psum_scatter(
        jnp.dot(row_block, in_weights, preferred_element_type=jnp.float32),
        "dp",
        scatter_dimension=0,
        tiled=True,
    )
    gate_pre = pre_sums[:, 0:unit_count]
    up_pre = pre_sums[:, unit_count : 2 * unit_count]
    activations = jax.nn.silu(gate_pre) * up_pre
    hidden_local = activations.astype(jnp.bfloat16)
    hidden_all = lax.all_gather(hidden_local, "dp", axis=0, tiled=True)
    row_block = hidden_all
    pieces = jnp.dot(row_block, weight_sets[0][2], preferred_element_type=jnp.float32)
    out_cols = lax.psum_scatter(pieces, "fsdp", scatter_dimension=0, tiled=True)
    states = state_cols.astype(jnp.float32)
    col_ids = jnp.arange(col_width, dtype=jnp.int32) + group_index * col_width
    logits = states + out_cols
    row_peak = jnp.max(logits, axis=1)
    logits_list = [logits]
    peaks = [row_peak]
    sums = [jnp.sum(jnp.exp(logits - row_peak[:, None]), axis=1)]
    picks = [jnp.sum(jnp.where(col_ids[None, :] == ids_all[:, None], logits, 0.0), axis=1)]
    row_peak, summed, picked = combined_all(
        (jnp.stack(peaks, axis=1), jnp.stack(sums, axis=1), jnp.stack(picks, axis=1)),
        "dp",
        combine_totals,
    )
    log_total = row_peak + jnp.log(summed)
    return (pre_sums, hidden_all, logits_list, log_total, picked - log_total)


def leave_one_out(log_gap, inside, prompt_index, rewards):
    divergence = lax.psum(jnp.sum(log_gap[:, None] * inside, axis=0), "fsdp")
    scores = rewards[0] - KL_WEIGHT * divergence
    same_prompt = (prompt_index[0][:, None] == prompt_index[0][None, :]).astype(jnp.float32)
    others = jnp.sum(same_prompt * scores[None, :], axis=1) - scores
    advantage = scores - others / (K - 1)
    weight = jnp.sum(inside * advantage[None, :], axis=1)
    return (advantage, weight)


def local(
    hidden_states,
    token_ids,
    norm_gain,
    ref_gate_w,
    ref_up_w,
    ref_down_w,
    pol_gate_w,
    pol_up_w,
    pol_down_w,
    sample_lengths,
    prompt_index,
    rewards,
):
    token_count = hidden_states.shape[0]
    model_width = hidden_states.shape[1]
    group_index = lax.axis_index("dp")
    member_index = lax.axis_index("fsdp")
    unit_count = pol_gate_w.shape[1]
    normed = normalize(hidden_states, norm_gain)
    normed_mixed, state_cols = (
        lax.all_to_all(normed, "dp", split_axis=1, concat_axis=0, tiled=True),
        lax.all_to_all(hidden_states, "dp", split_axis=1, concat_axis=0, tiled=True),
    )
    normed_cols = lax.all_gather(normed_mixed, "fsdp", axis=0, tiled=True)
    ids_all = lax.all_gather(token_ids, "dp", axis=0, tiled=True)
    own_start = group_index * token_count
    position = member_index * token_count + jnp.arange(token_count, dtype=jnp.int32)
    sample_ends = jnp.cumsum(sample_lengths[0])
    sample_starts = sample_ends - sample_lengths[0]
    inside = (
        (position[:, None] >= sample_starts[None, :]) & (position[:, None] < sample_ends[None, :])
    ).astype(jnp.float32)
    _, _, _, _, ref_lp = column_section(
        normed_cols, state_cols, ids_all, [(ref_gate_w, ref_up_w, ref_down_w)], group_index
    )
    ref_own = lax.dynamic_slice_in_dim(ref_lp[:, 0], own_start, token_count, 0)
    group_normed = lax.all_gather(normed, "fsdp", axis=0, tiled=True)
    row_block = group_normed
    gate_pre = jnp.dot(
        row_block,
        lax.all_gather(pol_gate_w, "dp", axis=0, tiled=True),
        preferred_element_type=jnp.float32,
    )
    up_pre = jnp.dot(
        row_block,
        lax.all_gather(pol_up_w, "dp", axis=0, tiled=True),
        preferred_element_type=jnp.float32,
    )
    down_full = lax.all_gather(pol_down_w, "dp", axis=1, tiled=True)
    hidden = (jax.nn.silu(gate_pre) * up_pre).astype(jnp.bfloat16)
    row_block = hidden
    pol_out = lax.psum_scatter(
        jnp.dot(row_block, down_full, preferred_element_type=jnp.float32),
        "fsdp",
        scatter_dimension=0,
        tiled=True,
    )
    logits = hidden_states.astype(jnp.float32) + pol_out
    row_peak = jnp.max(logits, axis=1)
    log_total = row_peak + jnp.log(jnp.sum(jnp.exp(logits - row_peak[:, None]), axis=1))
    columns = jnp.arange(model_width, dtype=jnp.int32)
    onehot = (columns[None, :] == token_ids[:, None]).astype(jnp.float32)
    pol_own = (
        jnp.sum(jnp.where(columns[None, :] == token_ids[:, None], logits, 0.0), axis=1) - log_total
    )
    advantage, weight = leave_one_out(pol_own - ref_own, inside, prompt_index, rewards)
    grad_logits = (-weight[:, None] * (onehot - jnp.exp(logits - log_total[:, None]))).astype(
        jnp.bfloat16
    )
    group_grads = lax.all_gather(grad_logits, "fsdp", axis=0, tiled=True)
    down_term = lax.dot_general(
        hidden, group_grads, (((0,), (0,)), ((), ())), preferred_element_type=jnp.float32
    )
    grad_down = lax.psum_scatter(
        down_term.astype(jnp.bfloat16), "dp", scatter_dimension=1, tiled=True
    ).astype(jnp.float32)
    grad_hidden = lax.dot_general(
        group_grads, down_full, (((1,), (1,)), ((), ())), preferred_element_type=jnp.float32
    )
    sigmoid_gate = jax.nn.sigmoid(gate_pre)
    grad_gate_pre = grad_hidden * up_pre * sigmoid_gate * (1.0 + gate_pre * (1.0 - sigmoid_gate))
    grad_up_pre = grad_hidden * gate_pre * sigmoid_gate
    gate_grads = jnp.concatenate(
        [grad_gate_pre.astype(jnp.bfloat16), grad_up_pre.astype(jnp.bfloat16)], axis=1
    )
    row_block = group_normed
    grad_inner = lax.psum_scatter(
        lax.dot_general(
            row_block, gate_grads, (((0,), (0,)), ((), ())), preferred_element_type=jnp.float32
        ).astype(jnp.bfloat16),
        "dp",
        scatter_dimension=0,
        tiled=True,
    ).astype(jnp.float32)
    return (grad_inner[:, :unit_count], grad_inner[:, unit_count:], grad_down, advantage[None, :])


def solution(mesh):
    members = mesh.shape["fsdp"]
    single = mesh.shape["dp"] == 1 and members > 1 and members & (members - 1) == 0
    return jax.shard_map(
        local_single if single else local,
        mesh=mesh,
        in_specs=(
            P(("dp", "fsdp"), None),
            P(("dp", "fsdp")),
            P(),
            P("dp", "fsdp"),
            P("dp", "fsdp"),
            P("fsdp", "dp"),
            P("dp", "fsdp"),
            P("dp", "fsdp"),
            P("fsdp", "dp"),
            P("dp", None),
            P("dp", None),
            P("dp", None),
        ),
        out_specs=(P("dp", "fsdp"), P("dp", "fsdp"), P("fsdp", "dp"), P("dp", None)),
        check_vma=False,
    )
```

```python
import functools

import jax
import jax.numpy as jnp
import numpy as np
from jax import lax
from jax.experimental import pallas as pl
from jax.experimental.pallas import tpu as pltpu
from jax.sharding import PartitionSpec as P

K = 8


EPSILON = 1e-06
KL_WEIGHT = 0.05
PIECES = 3
LANES = 128
FETCH_VMEM = 4 << 20
FORWARD_VMEM = 8 << 20
BACKWARD_VMEM = 32 << 20
BACKWARD_CHUNK = 1024


def exchange_levels(members):
    bits = [1 << b for b in range(members.bit_length() - 1)]
    levels, rest = [bits[:1]], bits[1:]
    while rest:
        low, rest = rest[:2], rest[2:]
        levels.append([low[0] | low[1], low[1], low[0]] if len(low) == 2 else low)
    return [level for level in levels if level]


def swap(values, mask):
    members = lax.axis_size("fsdp")
    return lax.ppermute(values, "fsdp", [(i, i ^ mask) for i in range(members)])


def tie(first, second):
    return lax.optimization_barrier((first, second))


def gather_blocks(rows, levels, beside=(None, None)):
    beside = list(beside)
    for level in reversed(levels[2:]):
        parts = [swap(rows, mask) for mask in level]
        if beside[0] is not None:
            parts, beside[0] = tie(parts, beside[0])
        rows = jnp.concatenate([rows] + parts, axis=0)
    blocks = [rows]
    if len(levels) > 1:
        blocks = blocks + [swap(rows, mask) for mask in levels[1]]
    if beside[1] is not None:
        blocks[1], beside[1] = tie(blocks[1], beside[1])
    return blocks + [swap(block, mask) for mask in levels[0] for block in blocks], beside


def scatter_rows(sums, levels):
    received = []
    for level in levels:
        for part in received:
            sums = sums + part.astype(jnp.float32)
        count = sums.shape[0] // (len(level) + 1)
        blocks = sums[count:].astype(jnp.bfloat16)
        received = [
            swap(blocks[place * count : (place + 1) * count], mask)
            for place, mask in enumerate(level)
        ]
        sums = sums[:count]
    return [sums] + received


def row_masks(levels):
    masks = np.zeros((1,), np.int32)
    for level in reversed(levels):
        masks = np.concatenate([masks] + [masks ^ mask for mask in level])
    return masks


def slope_kernel(parts, *refs):
    pol_parts, ref_parts = refs[:parts], refs[parts : 2 * parts]
    states_ref, ids, payload = refs[2 * parts :]
    count, width = states_ref.shape
    states = states_ref[...].astype(jnp.float32)
    chosen = lax.broadcasted_iota(jnp.int32, (count, width), 1) == ids[...]

    def token_logprob(terms):
        logits = states
        for term in terms:
            logits = logits + term[...].astype(jnp.float32)
        row_peak = jnp.max(logits, axis=1, keepdims=True)
        total = jnp.sum(jnp.exp(logits - row_peak), axis=1, keepdims=True)
        log_total = row_peak + jnp.log(total)
        picked = jnp.sum(jnp.where(chosen, logits, 0.0), axis=1, keepdims=True)
        return logits, log_total, picked - log_total

    logits, log_total, pol_lp = token_logprob(pol_parts)
    _, _, ref_lp = token_logprob(ref_parts)
    slopes = jnp.exp(logits - log_total) - jnp.where(chosen, 1.0, 0.0)
    payload[:, :width] = slopes.astype(jnp.bfloat16)
    lane = lax.broadcasted_iota(jnp.int32, (count, LANES), 1)
    rest = pol_lp - ref_lp
    extra = jnp.zeros((count, LANES), jnp.float32)
    for place in range(PIECES):
        piece = rest.astype(jnp.bfloat16).astype(jnp.float32)
        extra = jnp.where(lane == place, piece, extra)
        rest = rest - piece
    payload[:, width:] = extra.astype(jnp.bfloat16)


def slope_rows(pol_parts, ref_parts, states, ids):
    count, width = states.shape
    vmem = pl.BlockSpec(memory_space=pltpu.VMEM)
    return pl.pallas_call(
        functools.partial(slope_kernel, len(pol_parts)),
        out_shape=jax.ShapeDtypeStruct((count, width + LANES), jnp.bfloat16),
        in_specs=[vmem] * (2 * len(pol_parts) + 2),
        out_specs=vmem,
        compiler_params=pltpu.CompilerParams(vmem_limit_bytes=FETCH_VMEM),
    )(*pol_parts, *ref_parts, states, ids)


NT = (((1,), (1,)), ((), ()))
NN = (((1,), (0,)), ((), ()))


def column_chunk(width, wanted):
    return wanted if width % wanted == 0 else width


def dot(left, right, dims):
    return lax.dot_general(left, right, dims, preferred_element_type=jnp.float32)


def keep_in_hbm(array):
    return pltpu.with_memory_space_constraint(array, pltpu.HBM)


def fetch_kernel(*refs):
    count = len(refs) // 2
    sources, targets, sems = refs[:count], refs[count:-1], refs[-1]
    copies = [
        pltpu.make_async_copy(source, target, sems.at[place])
        for place, (source, target) in enumerate(zip(sources, targets))
    ]
    for copy in copies:
        copy.start()
    for copy in copies:
        copy.wait()


def fetch(weights):
    vmem = pl.BlockSpec(memory_space=pltpu.VMEM)
    hbm = pl.BlockSpec(memory_space=pltpu.HBM)
    return pl.pallas_call(
        fetch_kernel,
        out_shape=[jax.ShapeDtypeStruct(w.shape, w.dtype) for w in weights],
        in_specs=[hbm] * len(weights),
        out_specs=[vmem] * len(weights),
        scratch_shapes=[pltpu.SemaphoreType.DMA((len(weights),))],
        compiler_params=pltpu.CompilerParams(vmem_limit_bytes=FETCH_VMEM),
        cost_estimate=pl.CostEstimate(
            flops=0, bytes_accessed=sum(2 * w.size for w in weights), transcendentals=0
        ),
    )(*[keep_in_hbm(w) for w in weights])


def forward_model(weights, normed, hidden_rows, sent, kept):
    gate_w, up_w, down_w = weights
    half = kept.shape[0]
    gate = dot(gate_w[...], normed[...], NT)
    up = dot(up_w[...], normed[...], NT)
    hidden = gate * (1.0 / (1.0 + jnp.exp(-gate))) * up
    hidden_rows[...] = hidden.T.astype(jnp.bfloat16)

    part = dot(hidden_rows[...], down_w[...], NN)
    kept[...] = part[:half]
    sent[...] = part[half:].astype(jnp.bfloat16)
    return gate, up, hidden


def reference_kernel(block_count, *refs):
    blocks = refs[:block_count]
    gain, *weights = refs[block_count : block_count + 4]
    normed, sent, kept, hidden_rows = refs[block_count + 4 :]
    height = blocks[0].shape[0]
    for place, block in enumerate(blocks):
        values = block[...].astype(jnp.float32)
        factor = lax.rsqrt(jnp.mean(values * values, axis=1, keepdims=True) + EPSILON)
        normed[place * height : (place + 1) * height, :] = (values * factor * gain[...]).astype(
            jnp.bfloat16
        )
    forward_model(weights, normed, hidden_rows, sent, kept)


def policy_kernel(normed, *refs):
    weights = refs[:3]
    gate_out, up_out, hidden_out, sent, kept, hidden_rows = refs[3:]
    gate, up, hidden = forward_model(weights, normed, hidden_rows, sent, kept)
    gate_out[...] = gate
    up_out[...] = up
    hidden_out[...] = hidden.astype(jnp.bfloat16)


def forward_call(kernel, operands, extra, weights, tokens):
    units, width = weights[0].shape
    vmem = pl.BlockSpec(memory_space=pltpu.VMEM)
    shapes = extra + [
        jax.ShapeDtypeStruct((tokens // 2, width), jnp.bfloat16),
        jax.ShapeDtypeStruct((tokens // 2, width), jnp.float32),
    ]
    return pl.pallas_call(
        kernel,
        out_shape=shapes,
        in_specs=[vmem] * (len(operands) + 3),
        out_specs=[vmem] * len(shapes),
        scratch_shapes=[pltpu.VMEM((tokens, units), jnp.bfloat16)],
        compiler_params=pltpu.CompilerParams(vmem_limit_bytes=FORWARD_VMEM),
        cost_estimate=pl.CostEstimate(
            flops=6 * tokens * width * units,
            bytes_accessed=6 * units * width,
            transcendentals=tokens * units,
        ),
    )(*operands, *weights)


def forward_reference(blocks, gain, weights):
    width = blocks[0].shape[1]
    tokens = sum(block.shape[0] for block in blocks)
    return forward_call(
        functools.partial(reference_kernel, len(blocks)),
        blocks + [gain],
        [jax.ShapeDtypeStruct((tokens, width), jnp.bfloat16)],
        weights,
        tokens,
    )


def forward_policy(normed, weights):
    tokens, width = normed.shape
    units = weights[0].shape[0]
    return forward_call(
        policy_kernel,
        [normed],
        [jax.ShapeDtypeStruct((units, tokens), jnp.float32)] * 2
        + [jax.ShapeDtypeStruct((units, tokens), jnp.bfloat16)],
        weights,
        tokens,
    )


def backward_kernel(block_count, chunk, token_count, *refs):
    blocks = refs[:block_count]
    normed, gate_ref, up_ref, hidden_ref, lengths, prompts, rewards, masks, down = refs[
        block_count : block_count + 9
    ]
    grad_gate, grad_up, grad_down, advantage_out = refs[block_count + 9 : block_count + 13]
    slopes, gate_left, up_left, down_left, gate_buf, up_buf, down_buf, sems = refs[
        block_count + 13 :
    ]
    width = normed.shape[1]
    steps = width // chunk
    tokens = normed.shape[0]
    samples = lengths.shape[1]
    height = blocks[0].shape[0]

    def columns(step):
        return pl.ds(pl.multiple_of(step * chunk, chunk), chunk)

    def copy_out(which, step):
        source = (gate_buf, up_buf, down_buf)[which]
        target = (grad_gate, grad_up, grad_down)[which]
        return pltpu.make_async_copy(
            source.at[:, columns(step)], target.at[:, columns(step)], sems.at[which, step]
        )

    gaps = []
    for place, block in enumerate(blocks):
        slopes[place * height : (place + 1) * height, :] = block[:, :width]
        gaps.append(jnp.sum(block[:, width:].astype(jnp.float32), axis=1, keepdims=True))
    gap = jnp.concatenate(gaps, axis=0)

    row = lax.broadcasted_iota(jnp.int32, (samples, samples), 0)
    col = lax.broadcasted_iota(jnp.int32, (samples, samples), 1)
    diagonal = row == col

    def as_row(column):
        return jnp.sum(jnp.where(diagonal, column, 0.0), axis=0, keepdims=True)

    def as_column(line, mask):
        return jnp.sum(jnp.where(mask, line, 0.0), axis=1, keepdims=True)

    counts = lengths[...].astype(jnp.float32)
    ends = as_column(counts, col <= row)
    starts = ends - as_column(counts, diagonal)
    kinds = prompts[...].astype(jnp.float32)
    own = lax.axis_index("fsdp").astype(jnp.int32)
    within = lax.broadcasted_iota(jnp.int32, (1, tokens), 1) % token_count
    place_line = ((masks[...] ^ own) * token_count + within).astype(jnp.float32)
    token_row = lax.broadcasted_iota(jnp.int32, (tokens, tokens), 0)
    token_col = lax.broadcasted_iota(jnp.int32, (tokens, tokens), 1)
    place_column = as_column(place_line, token_row == token_col)

    def inside(position):
        return (position >= starts) & (position < ends)

    lane = lax.broadcasted_iota(jnp.int32, (1, tokens), 1).astype(jnp.float32)
    ordered = jnp.sum(jnp.where(place_column == lane, gap, 0.0), axis=0, keepdims=True)
    divergence = as_column(ordered, inside(lane))
    scores = as_column(rewards[...], diagonal) - KL_WEIGHT * divergence
    others = as_column(as_row(scores), as_column(kinds, diagonal) == kinds) - scores
    advantage = scores - others / (K - 1)
    advantage_out[...] = as_row(advantage)
    weight = jnp.sum(jnp.where(inside(place_line), advantage, 0.0), axis=0, keepdims=True)

    down_left[...] = (hidden_ref[...].astype(jnp.float32) * weight).astype(jnp.bfloat16)

    def product(which, left, right, buffer):
        def body(step, _):
            buffer[:, columns(step)] = dot(left[...], right[:, columns(step)], NN)
            copy_out(which, step).start()
            return 0

        return body

    early = steps - steps // 4
    down_step = product(2, down_left, slopes, down_buf)
    lax.fori_loop(0, early, down_step, 0)
    grad_hidden = dot(down[...], slopes[...], NT) * weight
    lax.fori_loop(early, steps, down_step, 0)
    gate = gate_ref[...]
    sigmoid = 1.0 / (1.0 + jnp.exp(-gate))
    gate_left[...] = (
        grad_hidden * up_ref[...] * sigmoid * (1.0 + gate * (1.0 - sigmoid))
    ).astype(jnp.bfloat16)
    up_left[...] = (grad_hidden * gate * sigmoid).astype(jnp.bfloat16)
    lax.fori_loop(0, steps, product(0, gate_left, normed, gate_buf), 0)
    lax.fori_loop(0, steps, product(1, up_left, normed, up_buf), 0)

    def finish(step, _):
        for which in range(3):
            copy_out(which, step).wait()
        return 0

    lax.fori_loop(0, steps, finish, 0)


def backward(blocks, normed, gate, up, hidden, samples, down, token_count):
    tokens, width = normed.shape
    units = gate.shape[0]
    chunk = column_chunk(width, BACKWARD_CHUNK)
    vmem = pl.BlockSpec(memory_space=pltpu.VMEM)
    hbm = pl.BlockSpec(memory_space=pl.ANY)
    grad = jax.ShapeDtypeStruct((units, width), jnp.float32)
    count = samples[0].shape[1]
    left = pltpu.VMEM((units, tokens), jnp.bfloat16)
    buffer = pltpu.VMEM((units, width), jnp.float32)
    steps = width // chunk
    return pl.pallas_call(
        functools.partial(backward_kernel, len(blocks), chunk, token_count),
        out_shape=(grad, grad, grad, jax.ShapeDtypeStruct((1, count), jnp.float32)),
        in_specs=[vmem] * (len(blocks) + 9),
        out_specs=(hbm, hbm, hbm, vmem),
        scratch_shapes=[
            pltpu.VMEM((tokens, width), jnp.bfloat16),
            left,
            left,
            left,
            buffer,
            buffer,
            buffer,
            pltpu.SemaphoreType.DMA((3, steps)),
        ],
        compiler_params=pltpu.CompilerParams(vmem_limit_bytes=BACKWARD_VMEM),
        cost_estimate=pl.CostEstimate(
            flops=8 * tokens * width * units,
            bytes_accessed=14 * units * width,
            transcendentals=tokens * units,
        ),
    )(
        *blocks,
        normed,
        gate,
        up,
        hidden,
        *samples,
        down,
    )


def local_single(
    hidden_states,
    token_ids,
    norm_gain,
    ref_gate_w,
    ref_up_w,
    ref_down_w,
    pol_gate_w,
    pol_up_w,
    pol_down_w,
    sample_lengths,
    prompt_index,
    rewards,
):
    token_count, width = hidden_states.shape
    levels = exchange_levels(lax.axis_size("fsdp"))
    row_members = jnp.asarray(np.repeat(row_masks(levels), token_count))

    blocks, (ref_weights, pol_weights) = gather_blocks(
        hidden_states,
        levels,
        (
            fetch([ref_gate_w.T, ref_up_w.T, ref_down_w]),
            fetch([pol_gate_w.T, pol_up_w.T, pol_down_w]),
        ),
    )
    normed, ref_sent, ref_kept = forward_reference(blocks, norm_gain[None, :], ref_weights)
    gate, up, hidden, pol_sent, pol_kept = forward_policy(normed, pol_weights)

    def reduce_rows(sent, kept):
        return scatter_rows(kept + swap(sent, levels[0][0]).astype(jnp.float32), levels[1:])

    ref_parts = reduce_rows(ref_sent, ref_kept)
    pol_parts = reduce_rows(pol_sent, pol_kept)
    payload = slope_rows(pol_parts, ref_parts, hidden_states, token_ids[:, None])
    slope_blocks, (_, down_again) = gather_blocks(payload, levels, (None, fetch([pol_down_w])))
    grad_gate, grad_up, grad_down, advantage = backward(
        slope_blocks,
        normed,
        gate,
        up,
        hidden,
        (sample_lengths, prompt_index, rewards, row_members[None, :]),
        down_again[0],
        token_count,
    )
    return grad_gate.T, grad_up.T, grad_down, advantage


def combined_all(part, axis, combine):
    gathered = jax.tree.map(lambda a: lax.all_gather(a, axis), part)

    def take(source):
        return jax.tree.map(lambda a: lax.dynamic_index_in_dim(a, source, 0, False), gathered)

    return lax.fori_loop(
        1, lax.axis_size(axis), lambda source, state: combine(state, take(source)), take(0)
    )


def normalize(states, norm_gain):
    values = states.astype(jnp.float32)
    factor = lax.rsqrt(jnp.mean(values * values, axis=-1, keepdims=True) + EPSILON)
    return (values * factor * norm_gain).astype(jnp.bfloat16)


def combine_totals(first, second):
    row_peak = jnp.maximum(first[0], second[0])
    summed = first[1] * jnp.exp(first[0] - row_peak) + second[1] * jnp.exp(second[0] - row_peak)
    return (row_peak, summed, first[2] + second[2])


def column_section(normed_cols, state_cols, ids_all, weight_sets, group_index):
    col_width = state_cols.shape[1]
    unit_count = weight_sets[0][0].shape[1]
    in_weights = jnp.concatenate(
        [matrix for triple in weight_sets for matrix in triple[:2]], axis=1
    )
    row_block = normed_cols
    pre_sums = lax.psum_scatter(
        jnp.dot(row_block, in_weights, preferred_element_type=jnp.float32),
        "dp",
        scatter_dimension=0,
        tiled=True,
    )
    gate_pre = pre_sums[:, 0:unit_count]
    up_pre = pre_sums[:, unit_count : 2 * unit_count]
    activations = jax.nn.silu(gate_pre) * up_pre
    hidden_local = activations.astype(jnp.bfloat16)
    hidden_all = lax.all_gather(hidden_local, "dp", axis=0, tiled=True)
    row_block = hidden_all
    pieces = jnp.dot(row_block, weight_sets[0][2], preferred_element_type=jnp.float32)
    out_cols = lax.psum_scatter(pieces, "fsdp", scatter_dimension=0, tiled=True)
    states = state_cols.astype(jnp.float32)
    col_ids = jnp.arange(col_width, dtype=jnp.int32) + group_index * col_width
    logits = states + out_cols
    row_peak = jnp.max(logits, axis=1)
    logits_list = [logits]
    peaks = [row_peak]
    sums = [jnp.sum(jnp.exp(logits - row_peak[:, None]), axis=1)]
    picks = [jnp.sum(jnp.where(col_ids[None, :] == ids_all[:, None], logits, 0.0), axis=1)]
    row_peak, summed, picked = combined_all(
        (jnp.stack(peaks, axis=1), jnp.stack(sums, axis=1), jnp.stack(picks, axis=1)),
        "dp",
        combine_totals,
    )
    log_total = row_peak + jnp.log(summed)
    return (pre_sums, hidden_all, logits_list, log_total, picked - log_total)


def leave_one_out(log_gap, inside, prompt_index, rewards):
    divergence = lax.psum(jnp.sum(log_gap[:, None] * inside, axis=0), "fsdp")
    scores = rewards[0] - KL_WEIGHT * divergence
    same_prompt = (prompt_index[0][:, None] == prompt_index[0][None, :]).astype(jnp.float32)
    others = jnp.sum(same_prompt * scores[None, :], axis=1) - scores
    advantage = scores - others / (K - 1)
    weight = jnp.sum(inside * advantage[None, :], axis=1)
    return (advantage, weight)


def local(
    hidden_states,
    token_ids,
    norm_gain,
    ref_gate_w,
    ref_up_w,
    ref_down_w,
    pol_gate_w,
    pol_up_w,
    pol_down_w,
    sample_lengths,
    prompt_index,
    rewards,
):
    token_count = hidden_states.shape[0]
    model_width = hidden_states.shape[1]
    group_index = lax.axis_index("dp")
    member_index = lax.axis_index("fsdp")
    unit_count = pol_gate_w.shape[1]
    normed = normalize(hidden_states, norm_gain)
    normed_mixed, state_cols = (
        lax.all_to_all(normed, "dp", split_axis=1, concat_axis=0, tiled=True),
        lax.all_to_all(hidden_states, "dp", split_axis=1, concat_axis=0, tiled=True),
    )
    normed_cols = lax.all_gather(normed_mixed, "fsdp", axis=0, tiled=True)
    ids_all = lax.all_gather(token_ids, "dp", axis=0, tiled=True)
    own_start = group_index * token_count
    position = member_index * token_count + jnp.arange(token_count, dtype=jnp.int32)
    sample_ends = jnp.cumsum(sample_lengths[0])
    sample_starts = sample_ends - sample_lengths[0]
    inside = (
        (position[:, None] >= sample_starts[None, :]) & (position[:, None] < sample_ends[None, :])
    ).astype(jnp.float32)
    _, _, _, _, ref_lp = column_section(
        normed_cols, state_cols, ids_all, [(ref_gate_w, ref_up_w, ref_down_w)], group_index
    )
    ref_own = lax.dynamic_slice_in_dim(ref_lp[:, 0], own_start, token_count, 0)
    group_normed = lax.all_gather(normed, "fsdp", axis=0, tiled=True)
    row_block = group_normed
    gate_pre = jnp.dot(
        row_block,
        lax.all_gather(pol_gate_w, "dp", axis=0, tiled=True),
        preferred_element_type=jnp.float32,
    )
    up_pre = jnp.dot(
        row_block,
        lax.all_gather(pol_up_w, "dp", axis=0, tiled=True),
        preferred_element_type=jnp.float32,
    )
    down_full = lax.all_gather(pol_down_w, "dp", axis=1, tiled=True)
    hidden = (jax.nn.silu(gate_pre) * up_pre).astype(jnp.bfloat16)
    row_block = hidden
    pol_out = lax.psum_scatter(
        jnp.dot(row_block, down_full, preferred_element_type=jnp.float32),
        "fsdp",
        scatter_dimension=0,
        tiled=True,
    )
    logits = hidden_states.astype(jnp.float32) + pol_out
    row_peak = jnp.max(logits, axis=1)
    log_total = row_peak + jnp.log(jnp.sum(jnp.exp(logits - row_peak[:, None]), axis=1))
    columns = jnp.arange(model_width, dtype=jnp.int32)
    onehot = (columns[None, :] == token_ids[:, None]).astype(jnp.float32)
    pol_own = (
        jnp.sum(jnp.where(columns[None, :] == token_ids[:, None], logits, 0.0), axis=1) - log_total
    )
    advantage, weight = leave_one_out(pol_own - ref_own, inside, prompt_index, rewards)
    grad_logits = (-weight[:, None] * (onehot - jnp.exp(logits - log_total[:, None]))).astype(
        jnp.bfloat16
    )
    group_grads = lax.all_gather(grad_logits, "fsdp", axis=0, tiled=True)
    down_term = lax.dot_general(
        hidden, group_grads, (((0,), (0,)), ((), ())), preferred_element_type=jnp.float32
    )
    grad_down = lax.psum_scatter(
        down_term.astype(jnp.bfloat16), "dp", scatter_dimension=1, tiled=True
    ).astype(jnp.float32)
    grad_hidden = lax.dot_general(
        group_grads, down_full, (((1,), (1,)), ((), ())), preferred_element_type=jnp.float32
    )
    sigmoid_gate = jax.nn.sigmoid(gate_pre)
    grad_gate_pre = grad_hidden * up_pre * sigmoid_gate * (1.0 + gate_pre * (1.0 - sigmoid_gate))
    grad_up_pre = grad_hidden * gate_pre * sigmoid_gate
    gate_grads = jnp.concatenate(
        [grad_gate_pre.astype(jnp.bfloat16), grad_up_pre.astype(jnp.bfloat16)], axis=1
    )
    row_block = group_normed
    grad_inner = lax.psum_scatter(
        lax.dot_general(
            row_block, gate_grads, (((0,), (0,)), ((), ())), preferred_element_type=jnp.float32
        ).astype(jnp.bfloat16),
        "dp",
        scatter_dimension=0,
        tiled=True,
    ).astype(jnp.float32)
    return (grad_inner[:, :unit_count], grad_inner[:, unit_count:], grad_down, advantage[None, :])


def solution(mesh):
    members = mesh.shape["fsdp"]
    single = mesh.shape["dp"] == 1 and members > 1 and members & (members - 1) == 0
    return jax.shard_map(
        local_single if single else local,
        mesh=mesh,
        in_specs=(
            P(("dp", "fsdp"), None),
            P(("dp", "fsdp")),
            P(),
            P("dp", "fsdp"),
            P("dp", "fsdp"),
            P("fsdp", "dp"),
            P("dp", "fsdp"),
            P("dp", "fsdp"),
            P("fsdp", "dp"),
            P("dp", None),
            P("dp", None),
            P("dp", None),
        ),
        out_specs=(P("dp", "fsdp"), P("dp", "fsdp"), P("fsdp", "dp"), P("dp", None)),
        check_vma=False,
    )
```

```python
import functools

import jax
import jax.numpy as jnp
import numpy as np
from jax import lax
from jax.experimental import pallas as pl
from jax.experimental.pallas import tpu as pltpu
from jax.sharding import PartitionSpec as P

K = 8


EPSILON = 1e-06
KL_WEIGHT = 0.05
PIECES = 3
LANES = 128
FETCH_VMEM = 4 << 20
FORWARD_VMEM = 8 << 20
BACKWARD_VMEM = 32 << 20
BACKWARD_CHUNK = 1024


def exchange_levels(members):
    bits = [1 << b for b in range(members.bit_length() - 1)]
    levels, rest = [bits[:1]], bits[1:]
    while rest:
        low, rest = rest[:2], rest[2:]
        both = low[0] | low[-1]
        group = [both, low[-1], low[0]] if len(levels) == 1 else [low[-1], both, low[0]]
        levels.append(group if len(low) == 2 else low)
    return [level for level in levels if level]


def swap(values, mask):
    members = lax.axis_size("fsdp")
    return lax.ppermute(values, "fsdp", [(i, i ^ mask) for i in range(members)])


def tie(first, second):
    return lax.optimization_barrier((first, second))


def gather_blocks(rows, levels, beside=(None, None)):
    beside = list(beside)
    for level in reversed(levels[2:]):
        parts = [swap(rows, mask) for mask in level]
        if beside[0] is not None:
            parts, beside[0] = tie(parts, beside[0])
        rows = jnp.concatenate([rows] + parts, axis=0)
    blocks = [rows]
    if len(levels) > 1:
        blocks = blocks + [swap(rows, mask) for mask in levels[1]]
    if beside[1] is not None:
        blocks[1], beside[1] = tie(blocks[1], beside[1])
    return blocks + [swap(block, mask) for mask in levels[0] for block in blocks], beside


def scatter_rows(sums, levels):
    received = []
    for level in levels:
        for part in received:
            sums = sums + part.astype(jnp.float32)
        count = sums.shape[0] // (len(level) + 1)
        blocks = sums[count:].astype(jnp.bfloat16)
        received = [
            swap(blocks[place * count : (place + 1) * count], mask)
            for place, mask in enumerate(level)
        ]
        sums = sums[:count]
    return [sums] + received


def row_masks(levels):
    masks = np.zeros((1,), np.int32)
    for level in reversed(levels):
        masks = np.concatenate([masks] + [masks ^ mask for mask in level])
    return masks


def slope_kernel(parts, *refs):
    pol_parts, ref_parts = refs[:parts], refs[parts : 2 * parts]
    states_ref, ids, payload = refs[2 * parts :]
    count, width = states_ref.shape
    states = states_ref[...].astype(jnp.float32)
    chosen = lax.broadcasted_iota(jnp.int32, (count, width), 1) == ids[...]

    def token_logprob(terms):
        logits = states
        for term in terms:
            logits = logits + term[...].astype(jnp.float32)
        row_peak = jnp.max(logits, axis=1, keepdims=True)
        total = jnp.sum(jnp.exp(logits - row_peak), axis=1, keepdims=True)
        log_total = row_peak + jnp.log(total)
        picked = jnp.sum(jnp.where(chosen, logits, 0.0), axis=1, keepdims=True)
        return logits, log_total, picked - log_total

    logits, log_total, pol_lp = token_logprob(pol_parts)
    _, _, ref_lp = token_logprob(ref_parts)
    slopes = jnp.exp(logits - log_total) - jnp.where(chosen, 1.0, 0.0)
    payload[:, :width] = slopes.astype(jnp.bfloat16)
    lane = lax.broadcasted_iota(jnp.int32, (count, LANES), 1)
    rest = pol_lp - ref_lp
    extra = jnp.zeros((count, LANES), jnp.float32)
    for place in range(PIECES):
        piece = rest.astype(jnp.bfloat16).astype(jnp.float32)
        extra = jnp.where(lane == place, piece, extra)
        rest = rest - piece
    payload[:, width:] = extra.astype(jnp.bfloat16)


def slope_rows(pol_parts, ref_parts, states, ids):
    count, width = states.shape
    vmem = pl.BlockSpec(memory_space=pltpu.VMEM)
    return pl.pallas_call(
        functools.partial(slope_kernel, len(pol_parts)),
        out_shape=jax.ShapeDtypeStruct((count, width + LANES), jnp.bfloat16),
        in_specs=[vmem] * (2 * len(pol_parts) + 2),
        out_specs=vmem,
        compiler_params=pltpu.CompilerParams(vmem_limit_bytes=FETCH_VMEM),
    )(*pol_parts, *ref_parts, states, ids)


NT = (((1,), (1,)), ((), ()))
NN = (((1,), (0,)), ((), ()))


def column_chunk(width, wanted):
    return wanted if width % wanted == 0 else width


def dot(left, right, dims):
    return lax.dot_general(left, right, dims, preferred_element_type=jnp.float32)


def keep_in_hbm(array):
    return pltpu.with_memory_space_constraint(array, pltpu.HBM)


def fetch_kernel(*refs):
    count = len(refs) // 2
    sources, targets, sems = refs[:count], refs[count:-1], refs[-1]
    copies = [
        pltpu.make_async_copy(source, target, sems.at[place])
        for place, (source, target) in enumerate(zip(sources, targets))
    ]
    for copy in copies:
        copy.start()
    for copy in copies:
        copy.wait()


def fetch(weights):
    vmem = pl.BlockSpec(memory_space=pltpu.VMEM)
    hbm = pl.BlockSpec(memory_space=pltpu.HBM)
    return pl.pallas_call(
        fetch_kernel,
        out_shape=[jax.ShapeDtypeStruct(w.shape, w.dtype) for w in weights],
        in_specs=[hbm] * len(weights),
        out_specs=[vmem] * len(weights),
        scratch_shapes=[pltpu.SemaphoreType.DMA((len(weights),))],
        compiler_params=pltpu.CompilerParams(vmem_limit_bytes=FETCH_VMEM),
        cost_estimate=pl.CostEstimate(
            flops=0, bytes_accessed=sum(2 * w.size for w in weights), transcendentals=0
        ),
    )(*[keep_in_hbm(w) for w in weights])


def forward_model(weights, normed, hidden_rows, sent, kept):
    gate_w, up_w, down_w = weights
    half = kept.shape[0]
    gate = dot(gate_w[...], normed[...], NT)
    up = dot(up_w[...], normed[...], NT)
    hidden = gate * (1.0 / (1.0 + jnp.exp(-gate))) * up
    hidden_rows[...] = hidden.T.astype(jnp.bfloat16)

    part = dot(hidden_rows[...], down_w[...], NN)
    kept[...] = part[:half]
    sent[...] = part[half:].astype(jnp.bfloat16)
    return gate, up, hidden


def reference_kernel(block_count, *refs):
    blocks = refs[:block_count]
    gain, *weights = refs[block_count : block_count + 4]
    normed, sent, kept, hidden_rows = refs[block_count + 4 :]
    height = blocks[0].shape[0]
    for place, block in enumerate(blocks):
        values = block[...].astype(jnp.float32)
        factor = lax.rsqrt(jnp.mean(values * values, axis=1, keepdims=True) + EPSILON)
        normed[place * height : (place + 1) * height, :] = (values * factor * gain[...]).astype(
            jnp.bfloat16
        )
    forward_model(weights, normed, hidden_rows, sent, kept)


def policy_kernel(normed, *refs):
    weights = refs[:3]
    gate_out, up_out, hidden_out, sent, kept, hidden_rows = refs[3:]
    gate, up, hidden = forward_model(weights, normed, hidden_rows, sent, kept)
    gate_out[...] = gate
    up_out[...] = up
    hidden_out[...] = hidden.astype(jnp.bfloat16)


def forward_call(kernel, operands, extra, weights, tokens):
    units, width = weights[0].shape
    vmem = pl.BlockSpec(memory_space=pltpu.VMEM)
    shapes = extra + [
        jax.ShapeDtypeStruct((tokens // 2, width), jnp.bfloat16),
        jax.ShapeDtypeStruct((tokens // 2, width), jnp.float32),
    ]
    return pl.pallas_call(
        kernel,
        out_shape=shapes,
        in_specs=[vmem] * (len(operands) + 3),
        out_specs=[vmem] * len(shapes),
        scratch_shapes=[pltpu.VMEM((tokens, units), jnp.bfloat16)],
        compiler_params=pltpu.CompilerParams(vmem_limit_bytes=FORWARD_VMEM),
        cost_estimate=pl.CostEstimate(
            flops=6 * tokens * width * units,
            bytes_accessed=6 * units * width,
            transcendentals=tokens * units,
        ),
    )(*operands, *weights)


def forward_reference(blocks, gain, weights):
    width = blocks[0].shape[1]
    tokens = sum(block.shape[0] for block in blocks)
    return forward_call(
        functools.partial(reference_kernel, len(blocks)),
        blocks + [gain],
        [jax.ShapeDtypeStruct((tokens, width), jnp.bfloat16)],
        weights,
        tokens,
    )


def forward_policy(normed, weights):
    tokens, width = normed.shape
    units = weights[0].shape[0]
    return forward_call(
        policy_kernel,
        [normed],
        [jax.ShapeDtypeStruct((units, tokens), jnp.float32)] * 2
        + [jax.ShapeDtypeStruct((units, tokens), jnp.bfloat16)],
        weights,
        tokens,
    )


def backward_kernel(block_count, chunk, token_count, *refs):
    blocks = refs[:block_count]
    normed, gate_ref, up_ref, hidden_ref, lengths, prompts, rewards, masks, down = refs[
        block_count : block_count + 9
    ]
    grad_gate, grad_up, grad_down, advantage_out = refs[block_count + 9 : block_count + 13]
    slopes, gate_left, up_left, down_left, gate_buf, up_buf, down_buf, sems = refs[
        block_count + 13 :
    ]
    width = normed.shape[1]
    steps = width // chunk
    tokens = normed.shape[0]
    samples = lengths.shape[1]
    height = blocks[0].shape[0]

    def columns(step):
        return pl.ds(pl.multiple_of(step * chunk, chunk), chunk)

    def copy_out(which, step):
        source = (gate_buf, up_buf, down_buf)[which]
        target = (grad_gate, grad_up, grad_down)[which]
        return pltpu.make_async_copy(
            source.at[:, columns(step)], target.at[:, columns(step)], sems.at[which, step]
        )

    gaps = []
    for place, block in enumerate(blocks):
        slopes[place * height : (place + 1) * height, :] = block[:, :width]
        gaps.append(jnp.sum(block[:, width:].astype(jnp.float32), axis=1, keepdims=True))
    gap = jnp.concatenate(gaps, axis=0)

    row = lax.broadcasted_iota(jnp.int32, (samples, samples), 0)
    col = lax.broadcasted_iota(jnp.int32, (samples, samples), 1)
    diagonal = row == col

    def as_row(column):
        return jnp.sum(jnp.where(diagonal, column, 0.0), axis=0, keepdims=True)

    def as_column(line, mask):
        return jnp.sum(jnp.where(mask, line, 0.0), axis=1, keepdims=True)

    counts = lengths[...].astype(jnp.float32)
    ends = as_column(counts, col <= row)
    starts = ends - as_column(counts, diagonal)
    kinds = prompts[...].astype(jnp.float32)
    own = lax.axis_index("fsdp").astype(jnp.int32)
    within = lax.broadcasted_iota(jnp.int32, (1, tokens), 1) % token_count
    place_line = ((masks[...] ^ own) * token_count + within).astype(jnp.float32)
    token_row = lax.broadcasted_iota(jnp.int32, (tokens, tokens), 0)
    token_col = lax.broadcasted_iota(jnp.int32, (tokens, tokens), 1)
    place_column = as_column(place_line, token_row == token_col)

    def inside(position):
        return (position >= starts) & (position < ends)

    lane = lax.broadcasted_iota(jnp.int32, (1, tokens), 1).astype(jnp.float32)
    ordered = jnp.sum(jnp.where(place_column == lane, gap, 0.0), axis=0, keepdims=True)
    divergence = as_column(ordered, inside(lane))
    scores = as_column(rewards[...], diagonal) - KL_WEIGHT * divergence
    others = as_column(as_row(scores), as_column(kinds, diagonal) == kinds) - scores
    advantage = scores - others / (K - 1)
    advantage_out[...] = as_row(advantage)
    weight = jnp.sum(jnp.where(inside(place_line), advantage, 0.0), axis=0, keepdims=True)

    down_left[...] = (hidden_ref[...].astype(jnp.float32) * weight).astype(jnp.bfloat16)

    def product(which, left, right, buffer):
        def body(step, _):
            buffer[:, columns(step)] = dot(left[...], right[:, columns(step)], NN)
            copy_out(which, step).start()
            return 0

        return body

    down_step = product(2, down_left, slopes, down_buf)
    lax.fori_loop(0, steps, down_step, 0)
    grad_hidden = dot(down[...], slopes[...], NT) * weight
    gate = gate_ref[...]
    sigmoid = 1.0 / (1.0 + jnp.exp(-gate))
    gate_left[...] = (
        grad_hidden * up_ref[...] * sigmoid * (1.0 + gate * (1.0 - sigmoid))
    ).astype(jnp.bfloat16)
    up_left[...] = (grad_hidden * gate * sigmoid).astype(jnp.bfloat16)
    lax.fori_loop(0, steps, product(0, gate_left, normed, gate_buf), 0)
    lax.fori_loop(0, steps, product(1, up_left, normed, up_buf), 0)

    def finish(step, _):
        for which in range(3):
            copy_out(which, step).wait()
        return 0

    lax.fori_loop(0, steps, finish, 0)


def backward(blocks, normed, gate, up, hidden, samples, down, token_count):
    tokens, width = normed.shape
    units = gate.shape[0]
    chunk = column_chunk(width, BACKWARD_CHUNK)
    vmem = pl.BlockSpec(memory_space=pltpu.VMEM)
    hbm = pl.BlockSpec(memory_space=pl.ANY)
    grad = jax.ShapeDtypeStruct((units, width), jnp.float32)
    count = samples[0].shape[1]
    left = pltpu.VMEM((units, tokens), jnp.bfloat16)
    buffer = pltpu.VMEM((units, width), jnp.float32)
    steps = width // chunk
    return pl.pallas_call(
        functools.partial(backward_kernel, len(blocks), chunk, token_count),
        out_shape=(grad, grad, grad, jax.ShapeDtypeStruct((1, count), jnp.float32)),
        in_specs=[vmem] * (len(blocks) + 9),
        out_specs=(hbm, hbm, hbm, vmem),
        scratch_shapes=[
            pltpu.VMEM((tokens, width), jnp.bfloat16),
            left,
            left,
            left,
            buffer,
            buffer,
            buffer,
            pltpu.SemaphoreType.DMA((3, steps)),
        ],
        compiler_params=pltpu.CompilerParams(vmem_limit_bytes=BACKWARD_VMEM),
        cost_estimate=pl.CostEstimate(
            flops=8 * tokens * width * units,
            bytes_accessed=14 * units * width,
            transcendentals=tokens * units,
        ),
    )(
        *blocks,
        normed,
        gate,
        up,
        hidden,
        *samples,
        down,
    )


def local_single(
    hidden_states,
    token_ids,
    norm_gain,
    ref_gate_w,
    ref_up_w,
    ref_down_w,
    pol_gate_w,
    pol_up_w,
    pol_down_w,
    sample_lengths,
    prompt_index,
    rewards,
):
    token_count, width = hidden_states.shape
    levels = exchange_levels(lax.axis_size("fsdp"))
    row_members = jnp.asarray(np.repeat(row_masks(levels), token_count))

    blocks, (ref_weights, pol_weights) = gather_blocks(
        hidden_states,
        levels,
        (
            fetch([ref_gate_w.T, ref_up_w.T, ref_down_w]),
            fetch([pol_gate_w.T, pol_up_w.T, pol_down_w]),
        ),
    )
    normed, ref_sent, ref_kept = forward_reference(blocks, norm_gain[None, :], ref_weights)
    gate, up, hidden, pol_sent, pol_kept = forward_policy(normed, pol_weights)

    def reduce_rows(sent, kept):
        return scatter_rows(kept + swap(sent, levels[0][0]).astype(jnp.float32), levels[1:])

    ref_parts = reduce_rows(ref_sent, ref_kept)
    pol_parts = reduce_rows(pol_sent, pol_kept)
    payload = slope_rows(pol_parts, ref_parts, hidden_states, token_ids[:, None])
    slope_blocks, (_, down_again) = gather_blocks(payload, levels, (None, fetch([pol_down_w])))
    grad_gate, grad_up, grad_down, advantage = backward(
        slope_blocks,
        normed,
        gate,
        up,
        hidden,
        (sample_lengths, prompt_index, rewards, row_members[None, :]),
        down_again[0],
        token_count,
    )
    return grad_gate.T, grad_up.T, grad_down, advantage


def combined_all(part, axis, combine):
    gathered = jax.tree.map(lambda a: lax.all_gather(a, axis), part)

    def take(source):
        return jax.tree.map(lambda a: lax.dynamic_index_in_dim(a, source, 0, False), gathered)

    return lax.fori_loop(
        1, lax.axis_size(axis), lambda source, state: combine(state, take(source)), take(0)
    )


def normalize(states, norm_gain):
    values = states.astype(jnp.float32)
    factor = lax.rsqrt(jnp.mean(values * values, axis=-1, keepdims=True) + EPSILON)
    return (values * factor * norm_gain).astype(jnp.bfloat16)


def combine_totals(first, second):
    row_peak = jnp.maximum(first[0], second[0])
    summed = first[1] * jnp.exp(first[0] - row_peak) + second[1] * jnp.exp(second[0] - row_peak)
    return (row_peak, summed, first[2] + second[2])


def column_section(normed_cols, state_cols, ids_all, weight_sets, group_index):
    col_width = state_cols.shape[1]
    unit_count = weight_sets[0][0].shape[1]
    in_weights = jnp.concatenate(
        [matrix for triple in weight_sets for matrix in triple[:2]], axis=1
    )
    row_block = normed_cols
    pre_sums = lax.psum_scatter(
        jnp.dot(row_block, in_weights, preferred_element_type=jnp.float32),
        "dp",
        scatter_dimension=0,
        tiled=True,
    )
    gate_pre = pre_sums[:, 0:unit_count]
    up_pre = pre_sums[:, unit_count : 2 * unit_count]
    activations = jax.nn.silu(gate_pre) * up_pre
    hidden_local = activations.astype(jnp.bfloat16)
    hidden_all = lax.all_gather(hidden_local, "dp", axis=0, tiled=True)
    row_block = hidden_all
    pieces = jnp.dot(row_block, weight_sets[0][2], preferred_element_type=jnp.float32)
    out_cols = lax.psum_scatter(pieces, "fsdp", scatter_dimension=0, tiled=True)
    states = state_cols.astype(jnp.float32)
    col_ids = jnp.arange(col_width, dtype=jnp.int32) + group_index * col_width
    logits = states + out_cols
    row_peak = jnp.max(logits, axis=1)
    logits_list = [logits]
    peaks = [row_peak]
    sums = [jnp.sum(jnp.exp(logits - row_peak[:, None]), axis=1)]
    picks = [jnp.sum(jnp.where(col_ids[None, :] == ids_all[:, None], logits, 0.0), axis=1)]
    row_peak, summed, picked = combined_all(
        (jnp.stack(peaks, axis=1), jnp.stack(sums, axis=1), jnp.stack(picks, axis=1)),
        "dp",
        combine_totals,
    )
    log_total = row_peak + jnp.log(summed)
    return (pre_sums, hidden_all, logits_list, log_total, picked - log_total)


def leave_one_out(log_gap, inside, prompt_index, rewards):
    divergence = lax.psum(jnp.sum(log_gap[:, None] * inside, axis=0), "fsdp")
    scores = rewards[0] - KL_WEIGHT * divergence
    same_prompt = (prompt_index[0][:, None] == prompt_index[0][None, :]).astype(jnp.float32)
    others = jnp.sum(same_prompt * scores[None, :], axis=1) - scores
    advantage = scores - others / (K - 1)
    weight = jnp.sum(inside * advantage[None, :], axis=1)
    return (advantage, weight)


def local(
    hidden_states,
    token_ids,
    norm_gain,
    ref_gate_w,
    ref_up_w,
    ref_down_w,
    pol_gate_w,
    pol_up_w,
    pol_down_w,
    sample_lengths,
    prompt_index,
    rewards,
):
    token_count = hidden_states.shape[0]
    model_width = hidden_states.shape[1]
    group_index = lax.axis_index("dp")
    member_index = lax.axis_index("fsdp")
    unit_count = pol_gate_w.shape[1]
    normed = normalize(hidden_states, norm_gain)
    normed_mixed, state_cols = (
        lax.all_to_all(normed, "dp", split_axis=1, concat_axis=0, tiled=True),
        lax.all_to_all(hidden_states, "dp", split_axis=1, concat_axis=0, tiled=True),
    )
    normed_cols = lax.all_gather(normed_mixed, "fsdp", axis=0, tiled=True)
    ids_all = lax.all_gather(token_ids, "dp", axis=0, tiled=True)
    own_start = group_index * token_count
    position = member_index * token_count + jnp.arange(token_count, dtype=jnp.int32)
    sample_ends = jnp.cumsum(sample_lengths[0])
    sample_starts = sample_ends - sample_lengths[0]
    inside = (
        (position[:, None] >= sample_starts[None, :]) & (position[:, None] < sample_ends[None, :])
    ).astype(jnp.float32)
    _, _, _, _, ref_lp = column_section(
        normed_cols, state_cols, ids_all, [(ref_gate_w, ref_up_w, ref_down_w)], group_index
    )
    ref_own = lax.dynamic_slice_in_dim(ref_lp[:, 0], own_start, token_count, 0)
    group_normed = lax.all_gather(normed, "fsdp", axis=0, tiled=True)
    row_block = group_normed
    gate_pre = jnp.dot(
        row_block,
        lax.all_gather(pol_gate_w, "dp", axis=0, tiled=True),
        preferred_element_type=jnp.float32,
    )
    up_pre = jnp.dot(
        row_block,
        lax.all_gather(pol_up_w, "dp", axis=0, tiled=True),
        preferred_element_type=jnp.float32,
    )
    down_full = lax.all_gather(pol_down_w, "dp", axis=1, tiled=True)
    hidden = (jax.nn.silu(gate_pre) * up_pre).astype(jnp.bfloat16)
    row_block = hidden
    pol_out = lax.psum_scatter(
        jnp.dot(row_block, down_full, preferred_element_type=jnp.float32),
        "fsdp",
        scatter_dimension=0,
        tiled=True,
    )
    logits = hidden_states.astype(jnp.float32) + pol_out
    row_peak = jnp.max(logits, axis=1)
    log_total = row_peak + jnp.log(jnp.sum(jnp.exp(logits - row_peak[:, None]), axis=1))
    columns = jnp.arange(model_width, dtype=jnp.int32)
    onehot = (columns[None, :] == token_ids[:, None]).astype(jnp.float32)
    pol_own = (
        jnp.sum(jnp.where(columns[None, :] == token_ids[:, None], logits, 0.0), axis=1) - log_total
    )
    advantage, weight = leave_one_out(pol_own - ref_own, inside, prompt_index, rewards)
    grad_logits = (-weight[:, None] * (onehot - jnp.exp(logits - log_total[:, None]))).astype(
        jnp.bfloat16
    )
    group_grads = lax.all_gather(grad_logits, "fsdp", axis=0, tiled=True)
    down_term = lax.dot_general(
        hidden, group_grads, (((0,), (0,)), ((), ())), preferred_element_type=jnp.float32
    )
    grad_down = lax.psum_scatter(
        down_term.astype(jnp.bfloat16), "dp", scatter_dimension=1, tiled=True
    ).astype(jnp.float32)
    grad_hidden = lax.dot_general(
        group_grads, down_full, (((1,), (1,)), ((), ())), preferred_element_type=jnp.float32
    )
    sigmoid_gate = jax.nn.sigmoid(gate_pre)
    grad_gate_pre = grad_hidden * up_pre * sigmoid_gate * (1.0 + gate_pre * (1.0 - sigmoid_gate))
    grad_up_pre = grad_hidden * gate_pre * sigmoid_gate
    gate_grads = jnp.concatenate(
        [grad_gate_pre.astype(jnp.bfloat16), grad_up_pre.astype(jnp.bfloat16)], axis=1
    )
    row_block = group_normed
    grad_inner = lax.psum_scatter(
        lax.dot_general(
            row_block, gate_grads, (((0,), (0,)), ((), ())), preferred_element_type=jnp.float32
        ).astype(jnp.bfloat16),
        "dp",
        scatter_dimension=0,
        tiled=True,
    ).astype(jnp.float32)
    return (grad_inner[:, :unit_count], grad_inner[:, unit_count:], grad_down, advantage[None, :])


def solution(mesh):
    members = mesh.shape["fsdp"]
    single = mesh.shape["dp"] == 1 and members > 1 and members & (members - 1) == 0
    return jax.shard_map(
        local_single if single else local,
        mesh=mesh,
        in_specs=(
            P(("dp", "fsdp"), None),
            P(("dp", "fsdp")),
            P(),
            P("dp", "fsdp"),
            P("dp", "fsdp"),
            P("fsdp", "dp"),
            P("dp", "fsdp"),
            P("dp", "fsdp"),
            P("fsdp", "dp"),
            P("dp", None),
            P("dp", None),
            P("dp", None),
        ),
        out_specs=(P("dp", "fsdp"), P("dp", "fsdp"), P("fsdp", "dp"), P("dp", None)),
        check_vma=False,
    )
```
